256 devices in a mesh: tm: 64 (over x, z, core), feat: 4 (over y).
Axes of the slice: x: 4, y: 4, z: 8, core: 2. Of those that a mesh axis runs over, the one named last changes fastest.
Arguments:
- features: bfloat16 [131072, 512], P('tm'), may hold values from -64 to 64
- seg_lengths: int32 [128], replicated, may hold values from 1 to 4096, 131072 in all
Outputs:
- koopman: float32 [512, 512], P('feat')
- lag_error: float32 [128, 131072], P('feat', 'tm')
The draws below stay inside these ranges and needn't reach their ends.
All inputs are finite; a program needn't handle non-finite values.
Results may differ from the reference program's by a relative error of at most 0.0037.
Values may be sent and summed in bfloat16 or wider, within the bound.
A program may use at most 64 MiB of HBM per device.

```python
import math
import jax
import jax.numpy as jnp
import numpy as np
from jax import lax

F = 512
LAG = 64
NC = 128
FR_DEV = 2048
FRAMES = 131072
NSEG = 128
SEG_MOST = 4096


def draw_features(key, part):
    key_noise, key_cols, key_rows, key_shift = jax.random.split(key, 4)
    total_rows = FRAMES + LAG
    noise_all = jax.random.normal(key_noise, (total_rows, F), jnp.float32)
    row_scale = jnp.exp(jax.random.uniform(key_rows, (FRAMES, 1), jnp.float32, math.log(0.4), math.log(4.0)))
    recent = noise_all[LAG:]
    mixed_rows = recent + 0.8 * noise_all[:FRAMES] + 0.6 * jnp.roll(recent, 1, axis=1) + 0.45 * jnp.roll(recent, 7, axis=1)
    col_scale = jnp.exp(jax.random.uniform(key_cols, (1, F), jnp.float32, math.log(0.35), math.log(3.5)))
    drift_part = (0.5 + jnp.arange(FRAMES, dtype=jnp.float32)[:, None] / FRAMES) * jax.random.normal(key_shift, (1, F), jnp.float32)
    values = row_scale * col_scale * mixed_rows + drift_part
    return jnp.clip(values, -64.0, 64.0).astype(jnp.bfloat16)


def profile(number_of, total, limit, lean):
    weights = [(1 << 20) // math.isqrt(rank ** lean) + 1 for rank in range(2, number_of + 1)]
    surplus, counts = total - limit - (number_of - 1), [1] * (number_of - 1)
    while surplus > 0:
        free = [i for i in range(number_of - 1) if counts[i] < limit]
        mass, budget = sum([weights[i] for i in free]), surplus
        for i in free:
            more = min(limit - counts[i], max(1, budget * weights[i] // mass), surplus)
            counts[i] = counts[i] + more
            surplus = surplus - more
    return np.array([limit] + counts)


def ragged(stream_key, amount, total, most, slope):
    if amount == 2:
        one = jax.random.randint(stream_key, (), max(1, total - most), min(most, total - 1) + 1)
        return jnp.stack([one, total - one])
    lengths = jnp.asarray(profile(amount, total, most, slope), jnp.int32)
    twos = (amount - 1) // 2
    donor, sink = lengths[1:1 + 2 * twos:2], lengths[2:2 + 2 * twos:2]
    slack = jnp.minimum(donor - 1, most - sink)
    passed = jax.random.randint(jax.random.fold_in(stream_key, 1), (twos,), 0, 1 << 20) % (slack + 1)
    lengths = lengths.at[1:1 + 2 * twos:2].set(donor - passed).at[2:2 + 2 * twos:2].set(sink + passed)
    return lengths[jax.random.permutation(jax.random.fold_in(stream_key, 2), amount)]


def setup_inputs(seed: int = 0) -> dict:
    seeds = jax.random.split(jax.random.key(seed), 3)
    features = draw_features(jax.random.fold_in(seeds[2], 71), 0)
    seg_lengths = ragged(seeds[1], NSEG, FRAMES, SEG_MOST, 2).astype(jnp.int32)
    return {"features": features, "seg_lengths": seg_lengths}


RIDGE = 0.05

def reference(features, seg_lengths):
    frame_count = features.shape[0]
    feat_width = features.shape[1]
    seg_ends = jnp.cumsum(seg_lengths).astype(jnp.int32)
    moments = jnp.arange(frame_count, dtype=jnp.int32)
    later_seg = jnp.searchsorted(seg_ends, moments + LAG, side='right').astype(jnp.int32)
    now_seg = jnp.searchsorted(seg_ends, moments, side='right').astype(jnp.int32)
    validity = (later_seg == now_seg).astype(jnp.float32)
    pair_count = jnp.sum(jnp.maximum(seg_lengths - LAG, 0)).astype(jnp.float32)
    ahead_rows = jnp.concatenate([features[LAG:], jnp.zeros((LAG, feat_width), features.dtype)], axis=0)
    block_count = frame_count // FR_DEV
    highest = lax.Precision.HIGHEST

    def accumulate(totals, pieces):
        lead_rows, later_rows, mask_rows = pieces
        lead_rows = lead_rows.astype(jnp.float32)
        later_rows = later_rows.astype(jnp.float32)
        weights = mask_rows[:, None]
        gram_a = jnp.dot(lead_rows.T, weights * lead_rows, precision=highest) + jnp.dot(later_rows.T, weights * later_rows, precision=highest)
        gram_b = jnp.dot(lead_rows.T, weights * later_rows, precision=highest) + jnp.dot(later_rows.T, weights * lead_rows, precision=highest)
        sum_a = jnp.sum(weights * lead_rows, axis=0)
        sum_b = jnp.sum(weights * later_rows, axis=0)
        return ((totals[0] + gram_a, totals[1] + gram_b, totals[2] + sum_a, totals[3] + sum_b), None)
    square_zero = jnp.zeros((feat_width, feat_width), jnp.float32)
    vector_zero = jnp.zeros((feat_width,), jnp.float32)
    stacked = (features.reshape(block_count, FR_DEV, feat_width), ahead_rows.reshape(block_count, FR_DEV, feat_width), validity.reshape(block_count, FR_DEV))
    (gram_a, gram_b, sum_a, sum_b), _ = lax.scan(accumulate, (square_zero, square_zero, vector_zero, vector_zero), stacked)
    mean_vec = (sum_a + sum_b) / (2.0 * pair_count)
    outer_mean = jnp.outer(mean_vec, mean_vec)
    inst_cov = gram_a / (2.0 * pair_count) - outer_mean
    shifted = inst_cov + RIDGE * (jnp.trace(inst_cov) / feat_width) * jnp.eye(feat_width, dtype=jnp.float32)
    lag_cov = gram_b / (2.0 * pair_count) - outer_mean
    lower_chol = jnp.linalg.cholesky(shifted)
    half_solve = jax.scipy.linalg.solve_triangular(lower_chol, lag_cov, lower=True)
    koopman = jax.scipy.linalg.solve_triangular(lower_chol, half_solve.T, lower=True).T
    unit_basis = jnp.eye(feat_width, dtype=jnp.float32)[:, :NC]
    first_map = jax.scipy.linalg.solve_triangular(lower_chol.T, unit_basis, lower=False).astype(jnp.bfloat16)
    second_map = jax.scipy.linalg.solve_triangular(lower_chol.T, koopman[:, :NC], lower=False).astype(jnp.bfloat16)
    offset = jnp.dot(mean_vec, first_map.astype(jnp.float32) - second_map.astype(jnp.float32), precision=highest)
    lag_resid = jnp.dot(ahead_rows.astype(jnp.float32), first_map.astype(jnp.float32), preferred_element_type=jnp.float32) - jnp.dot(features.astype(jnp.float32), second_map.astype(jnp.float32), preferred_element_type=jnp.float32) - offset[None, :]
    lag_error = (lag_resid * validity[:, None]).T
    return (koopman, lag_error)
```

```python
import jax
import jax.numpy as jnp
from jax import lax
from jax.experimental import pallas as pl
from jax.experimental.pallas import tpu as pltpu
from jax.sharding import PartitionSpec as P

LAG = 64
NC = 128

RIDGE = 0.05
HIGHEST = lax.Precision.HIGHEST
LEAF = 128


def from_behind(shard, axis, by):
    count = lax.axis_size(axis)
    pairs = [(i, i + by) for i in range(count) if 0 <= i + by < count]
    return lax.ppermute(shard, axis, pairs)


def contract(left_rows, right_rows):
    return lax.dot_general(
        left_rows, right_rows, (((0,), (0,)), ((), ())), preferred_element_type=jnp.float32
    )


def exact_dot(left, right, left_dim=1, right_dim=0):
    return lax.dot_general(
        left,
        right,
        (((left_dim,), (right_dim,)), ((), ())),
        precision=HIGHEST,
        preferred_element_type=jnp.float32,
    )


def leaf_inverse(square):
    tiles = [square[8 * i : 8 * i + 8, :] for i in range(LEAF // 8)]
    lanes = lax.broadcasted_iota(jnp.int32, (8, LEAF), 1)
    subs = lax.broadcasted_iota(jnp.int32, (8, LEAF), 0)
    for j in range(LEAF - 1):
        own, sub = j // 8, j % 8
        row = jnp.broadcast_to(tiles[own][sub : sub + 1, :], (8, LEAF))
        pivot = jnp.broadcast_to(row[:, j : j + 1], (8, LEAF))
        at_pivot = lanes == j
        row = jnp.where(at_pivot, 1.0, row) / pivot
        for i in range(own, LEAF // 8):
            if i == own and sub == 7:
                continue
            factor = jnp.broadcast_to(tiles[i][:, j : j + 1], (8, LEAF))
            updated = jnp.where(at_pivot, 0.0, tiles[i]) - factor * row
            if i == own:
                updated = jnp.where(subs > sub, updated, tiles[i])
            tiles[i] = updated
    outs = []
    for i in range(LEAF // 8):
        rows = subs + 8 * i
        diag = jnp.sum(jnp.where(lanes == rows, tiles[i], 0.0), axis=1, keepdims=True)
        unit = jnp.where(lanes < rows, tiles[i], jnp.where(lanes == rows, 1.0, 0.0))
        outs.append(unit * lax.rsqrt(diag))
    return jnp.concatenate(outs, axis=0)


def whiten_kernel(
    index_ref, lengths_ref, moments_ref, sums_ref, koop_ref, first_ref, second_ref, offset_ref, work, cov
):
    feat_width = work.shape[0]
    blocks = feat_width // LEAF
    part = koop_ref.shape[0]
    pairs = jnp.maximum(lengths_ref[...] - LAG, 0).astype(jnp.float32)
    scale = 1.0 / (2.0 * jnp.sum(pairs, axis=1, keepdims=True))
    mean = sums_ref[0:1, :] * scale
    mean_cols = jnp.broadcast_to(mean, (LEAF, feat_width)).T
    rows_io = lax.broadcasted_iota(jnp.int32, (LEAF, LEAF), 0)
    lanes_io = lax.broadcasted_iota(jnp.int32, (LEAF, LEAF), 1)
    eye = rows_io == lanes_io
    trace = jnp.zeros((1, 1), jnp.float32)
    for k in range(blocks):
        square = moments_ref[2 * LEAF * k : 2 * LEAF * k + LEAF, LEAF * k : LEAF * k + LEAF]
        square = square * scale - mean_cols[LEAF * k : LEAF * k + LEAF, :] * mean[:, LEAF * k : LEAF * k + LEAF]
        diag = jnp.sum(jnp.where(eye, square, 0.0), axis=0, keepdims=True)
        trace = trace + jnp.sum(diag, axis=1, keepdims=True)
    ridge = RIDGE * (trace / feat_width)
    for k in range(blocks):
        for m in range(blocks):
            outer = mean_cols[LEAF * k : LEAF * k + LEAF, :] * mean[:, LEAF * m : LEAF * m + LEAF]
            block = moments_ref[2 * LEAF * k : 2 * LEAF * k + LEAF, LEAF * m : LEAF * m + LEAF] * scale - outer
            if k == m:
                block = block + jnp.where(eye, ridge, 0.0)
            work[LEAF * k : LEAF * k + LEAF, LEAF * m : LEAF * m + LEAF] = block
            straight = moments_ref[
                2 * LEAF * k + LEAF : 2 * LEAF * k + 2 * LEAF, LEAF * m : LEAF * m + LEAF
            ]
            turned = moments_ref[
                2 * LEAF * m + LEAF : 2 * LEAF * m + 2 * LEAF, LEAF * k : LEAF * k + LEAF
            ].T
            cov[LEAF * k : LEAF * k + LEAF, LEAF * m : LEAF * m + LEAF] = (straight + turned) * scale - outer

    def eliminate(k, carry):
        start = pl.multiple_of(k * LEAF, LEAF)
        inverse = leaf_inverse(work[pl.ds(start, LEAF), pl.ds(start, LEAF)])
        work[pl.ds(start, LEAF), pl.ds(start, LEAF)] = jnp.where(eye, 1.0, 0.0)
        panel = exact_dot(inverse, work[pl.ds(start, LEAF), :])
        wide_lanes = lax.broadcasted_iota(jnp.int32, (LEAF, feat_width), 1)
        below = jnp.where(wide_lanes >= start + LEAF, panel, 0.0)
        change = exact_dot(below, panel, 0, 0)
        in_block = (wide_lanes >= start) & (wide_lanes < start + LEAF)
        for i in range(blocks):
            old = work[LEAF * i : LEAF * i + LEAF, :]
            old = jnp.where(in_block & (k < i), 0.0, old)
            work[LEAF * i : LEAF * i + LEAF, :] = old - change[LEAF * i : LEAF * i + LEAF, :]
        work[pl.ds(start, LEAF), :] = panel
        return carry

    lax.fori_loop(0, blocks, eliminate, 0)
    rows_io = lax.broadcasted_iota(jnp.int32, (feat_width, feat_width), 0)
    lanes_io = lax.broadcasted_iota(jnp.int32, (feat_width, feat_width), 1)
    work[...] = jnp.where(rows_io >= lanes_io, work[...], 0.0)
    index = index_ref[0]
    comps = first_ref.shape[0]
    own_rows = work[pl.ds(pl.multiple_of(index * part, part), part), :]
    own_comps = work[pl.ds(pl.multiple_of(index * comps, comps), comps), :]
    stacked = jnp.concatenate([own_rows, own_comps], axis=0)
    koop = exact_dot(exact_dot(stacked, cov[...]), work[...], 1, 1)
    koop_ref[...] = koop[:part, :]
    first = own_comps.astype(jnp.bfloat16)
    second = exact_dot(koop[part:, :], work[...]).astype(jnp.bfloat16)
    first_ref[...] = first
    second_ref[...] = second
    gap = (first.astype(jnp.float32) - second.astype(jnp.float32)) * mean
    offset_ref[...] = jnp.broadcast_to(jnp.sum(gap, axis=1, keepdims=True), offset_ref.shape)


def whiten(index, lengths, moments, sums, part, comps):
    feat_width = moments.shape[1]
    vmem = pl.BlockSpec(memory_space=pltpu.VMEM)
    return pl.pallas_call(
        whiten_kernel,
        out_shape=(
            jax.ShapeDtypeStruct((part, feat_width), jnp.float32),
            jax.ShapeDtypeStruct((comps, feat_width), jnp.bfloat16),
            jax.ShapeDtypeStruct((comps, feat_width), jnp.bfloat16),
            jax.ShapeDtypeStruct((comps, 128), jnp.float32),
        ),
        in_specs=[pl.BlockSpec(memory_space=pltpu.SMEM), vmem, vmem, vmem],
        out_specs=(vmem, vmem, vmem, vmem),
        scratch_shapes=[
            pltpu.VMEM((feat_width, feat_width), jnp.float32),
            pltpu.VMEM((feat_width, feat_width), jnp.float32),
        ],
        name="whiten",
    )(index, lengths, moments, sums)


def shards(features, seg_lengths):
    frame_rows = features.shape[0]
    feat_width = features.shape[1]
    feat_count = lax.axis_size("feat")
    tm_index = lax.axis_index("tm")
    feat_index = lax.axis_index("feat")
    col_block = feat_width // feat_count
    comp_block = NC // feat_count
    tail_part = from_behind(features[:LAG], "tm", -1)
    ahead_rows = jnp.concatenate([features[LAG:], tail_part], axis=0)
    seg_ends = jnp.cumsum(seg_lengths).astype(jnp.int32)
    moments = tm_index * frame_rows - LAG + jnp.arange(frame_rows + LAG, dtype=jnp.int32)
    inside = (seg_ends[:, None] > moments[None, :]) & (seg_ends[:, None] <= moments[None, :] + LAG)
    clear = jnp.logical_not(jnp.any(inside, axis=0)) & (moments >= 0)
    valid_wide = clear.astype(jnp.float32)
    validity = valid_wide[LAG:]
    uses = (validity + valid_wide[:frame_rows]).astype(jnp.bfloat16)
    start_col = feat_index * col_block
    lead_cols = lax.dynamic_slice_in_dim(features, start_col, col_block, 1)
    gram_rows = contract(lead_cols * uses[:, None], features)
    cross_rows = contract(lead_cols * validity.astype(jnp.bfloat16)[:, None], ahead_rows)
    sums = jnp.dot(uses, features, preferred_element_type=jnp.float32)
    packed = jnp.concatenate(
        [gram_rows, cross_rows, jnp.broadcast_to(sums[None, :], (8, feat_width))], axis=0
    )
    packed = lax.psum(packed, "tm")
    gathered = lax.all_gather(packed[: 2 * col_block], "feat", axis=0, tiled=True)
    koopman_rows, first_part, second_part, offset = whiten(
        feat_index.astype(jnp.int32).reshape(1),
        seg_lengths.reshape(1, -1),
        gathered,
        packed[2 * col_block :],
        col_block,
        comp_block,
    )
    forward = jnp.einsum("cf,tf->ct", first_part, ahead_rows, preferred_element_type=jnp.float32)
    backward = jnp.einsum("cf,tf->ct", second_part, features, preferred_element_type=jnp.float32)
    lag_error = (forward - backward - offset[:, :1]) * validity[None, :]
    return (koopman_rows, lag_error)


def solution(mesh):
    in_specs = (P("tm", None), P())
    out_specs = (P("feat", None), P("feat", "tm"))
    return jax.shard_map(shards, mesh=mesh, in_specs=in_specs, out_specs=out_specs, check_vma=False)
```

```python
import jax
import jax.numpy as jnp
from jax import lax
from jax.experimental import pallas as pl
from jax.experimental.pallas import tpu as pltpu
from jax.sharding import PartitionSpec as P

LAG = 64
NC = 128

RIDGE = 0.05
HIGHEST = lax.Precision.HIGHEST
LEAF = 128
MESH = pl.DeviceIdType.MESH
X_CHIPS, Y_CHIPS, Z_CHIPS, CORES = 4, 4, 8, 2


def from_behind(shard, axis, by):
    count = lax.axis_size(axis)
    pairs = [(i, i + by) for i in range(count) if 0 <= i + by < count]
    return lax.ppermute(shard, axis, pairs)


def contract(left_rows, right_rows):
    return lax.dot_general(
        left_rows, right_rows, (((0,), (0,)), ((), ())), preferred_element_type=jnp.float32
    )


def exact_dot(left, right, left_dim=1, right_dim=0):
    return lax.dot_general(
        left,
        right,
        (((left_dim,), (right_dim,)), ((), ())),
        precision=HIGHEST,
        preferred_element_type=jnp.float32,
    )


def leaf_inverse(square):
    tiles = [square[8 * i : 8 * i + 8, :] for i in range(LEAF // 8)]
    lanes = lax.broadcasted_iota(jnp.int32, (8, LEAF), 1)
    subs = lax.broadcasted_iota(jnp.int32, (8, LEAF), 0)
    for j in range(LEAF - 1):
        own, sub = j // 8, j % 8
        row = jnp.broadcast_to(tiles[own][sub : sub + 1, :], (8, LEAF))
        pivot = jnp.broadcast_to(row[:, j : j + 1], (8, LEAF))
        at_pivot = lanes == j
        row = jnp.where(at_pivot, 1.0, row) / pivot
        for i in range(own, LEAF // 8):
            if i == own and sub == 7:
                continue
            factor = jnp.broadcast_to(tiles[i][:, j : j + 1], (8, LEAF))
            updated = jnp.where(at_pivot, 0.0, tiles[i]) - factor * row
            if i == own:
                updated = jnp.where(subs > sub, updated, tiles[i])
            tiles[i] = updated
    outs = []
    for i in range(LEAF // 8):
        rows = subs + 8 * i
        diag = jnp.sum(jnp.where(lanes == rows, tiles[i], 0.0), axis=1, keepdims=True)
        unit = jnp.where(lanes < rows, tiles[i], jnp.where(lanes == rows, 1.0, 0.0))
        outs.append(unit * lax.rsqrt(diag))
    return jnp.concatenate(outs, axis=0)


def whiten_kernel(
    index_ref, lengths_ref, moments_ref, koop_ref, first_ref, second_ref, offset_ref, work, cov
):
    feat_width = work.shape[0]
    blocks = feat_width // LEAF
    part = koop_ref.shape[0]
    pairs = jnp.maximum(lengths_ref[...] - LAG, 0).astype(jnp.float32)
    scale = 1.0 / (2.0 * jnp.sum(pairs, axis=1, keepdims=True))

    def moment(kind, k, m):
        top, left = LEAF * (2 * k + kind), LEAF * (m % 2)
        return moments_ref[m // 2, top : top + LEAF, left : left + LEAF]

    def gram_block(k, m):
        return moment(0, m, k).T if m == (k + blocks - 1) % blocks else moment(0, k, m)

    sums = moment(0, 0, blocks - 1)
    mean = jnp.concatenate([sums[m : m + 1, :] for m in range(blocks)], axis=1) * scale
    mean_cols = jnp.broadcast_to(mean, (LEAF, feat_width)).T
    rows_io = lax.broadcasted_iota(jnp.int32, (LEAF, LEAF), 0)
    lanes_io = lax.broadcasted_iota(jnp.int32, (LEAF, LEAF), 1)
    eye = rows_io == lanes_io
    trace = jnp.zeros((1, 1), jnp.float32)
    for k in range(blocks):
        square = gram_block(k, k) * scale - mean_cols[LEAF * k : LEAF * k + LEAF, :] * mean[:, LEAF * k : LEAF * k + LEAF]
        diag = jnp.sum(jnp.where(eye, square, 0.0), axis=0, keepdims=True)
        trace = trace + jnp.sum(diag, axis=1, keepdims=True)
    ridge = RIDGE * (trace / feat_width)
    for k in range(blocks):
        for m in range(blocks):
            outer = mean_cols[LEAF * k : LEAF * k + LEAF, :] * mean[:, LEAF * m : LEAF * m + LEAF]
            block = gram_block(k, m) * scale - outer
            if k == m:
                block = block + jnp.where(eye, ridge, 0.0)
            work[LEAF * k : LEAF * k + LEAF, LEAF * m : LEAF * m + LEAF] = block
            straight = moment(1, k, m)
            turned = moment(1, m, k).T
            cov[LEAF * k : LEAF * k + LEAF, LEAF * m : LEAF * m + LEAF] = (straight + turned) * scale - outer

    def eliminate(k, carry):
        start = pl.multiple_of(k * LEAF, LEAF)
        inverse = leaf_inverse(work[pl.ds(start, LEAF), pl.ds(start, LEAF)])
        work[pl.ds(start, LEAF), pl.ds(start, LEAF)] = jnp.where(eye, 1.0, 0.0)
        panel = exact_dot(inverse, work[pl.ds(start, LEAF), :])
        wide_lanes = lax.broadcasted_iota(jnp.int32, (LEAF, feat_width), 1)
        below = jnp.where(wide_lanes >= start + LEAF, panel, 0.0)
        change = exact_dot(below, panel, 0, 0)
        in_block = (wide_lanes >= start) & (wide_lanes < start + LEAF)
        for i in range(blocks):
            old = work[LEAF * i : LEAF * i + LEAF, :]
            old = jnp.where(in_block & (k < i), 0.0, old)
            work[LEAF * i : LEAF * i + LEAF, :] = old - change[LEAF * i : LEAF * i + LEAF, :]
        work[pl.ds(start, LEAF), :] = panel
        return carry

    lax.fori_loop(0, blocks, eliminate, 0)
    rows_io = lax.broadcasted_iota(jnp.int32, (feat_width, feat_width), 0)
    lanes_io = lax.broadcasted_iota(jnp.int32, (feat_width, feat_width), 1)
    work[...] = jnp.where(rows_io >= lanes_io, work[...], 0.0)
    index = index_ref[0]
    comps = first_ref.shape[0]
    own_rows = work[pl.ds(pl.multiple_of(index * part, part), part), :]
    own_comps = work[pl.ds(pl.multiple_of(index * comps, comps), comps), :]
    stacked = jnp.concatenate([own_rows, own_comps], axis=0)
    koop = exact_dot(exact_dot(stacked, cov[...]), work[...], 1, 1)
    koop_ref[...] = koop[:part, :]
    first = own_comps.astype(jnp.bfloat16)
    second = exact_dot(koop[part:, :], work[...]).astype(jnp.bfloat16)
    first_ref[...] = first
    second_ref[...] = second
    gap = (first.astype(jnp.float32) - second.astype(jnp.float32)) * mean
    offset_ref[...] = jnp.broadcast_to(jnp.sum(gap, axis=1, keepdims=True), offset_ref.shape)


def whiten(index, lengths, moments, part, comps):
    feat_width = 2 * moments.shape[2]
    vmem = pl.BlockSpec(memory_space=pltpu.VMEM)
    return pl.pallas_call(
        whiten_kernel,
        out_shape=(
            jax.ShapeDtypeStruct((part, feat_width), jnp.float32),
            jax.ShapeDtypeStruct((comps, feat_width), jnp.bfloat16),
            jax.ShapeDtypeStruct((comps, feat_width), jnp.bfloat16),
            jax.ShapeDtypeStruct((comps, 128), jnp.float32),
        ),
        in_specs=[pl.BlockSpec(memory_space=pltpu.SMEM), vmem, vmem],
        out_specs=(vmem, vmem, vmem, vmem),
        scratch_shapes=[
            pltpu.VMEM((feat_width, feat_width), jnp.float32),
            pltpu.VMEM((feat_width, feat_width), jnp.float32),
        ],
        name="whiten",
    )(index, lengths, moments)


def total_kernel(
    mine_ref, out_ref, from_core, held, from_x, from_z, core_send, core_recv, x_send, x_recv, z_send, z_recv,
    gz_send, gz_recv, ga_send, ga_recv, gb_send, gb_recv, gc_send, gc_recv
):
    place, y = lax.axis_index("tm"), lax.axis_index("feat")
    core = lax.rem(place, CORES)
    z = lax.rem(lax.div(place, CORES), Z_CHIPS)
    x = lax.div(place, CORES * Z_CHIPS)
    rows, half = held.shape
    x_rows = rows // X_CHIPS
    z_rows = x_rows // Z_CHIPS
    split = x_rows // 2

    def at(x_to, z_to, core_to):
        return {"tm": (x_to * Z_CHIPS + z_to) * CORES + core_to}

    def along_x(step):
        return at(lax.rem(x + step, X_CHIPS), z, core)

    def along_z(step):
        return at(x, lax.rem(z + step, Z_CHIPS), core)

    def along_y(step):
        return {"feat": lax.rem(y + step, Y_CHIPS)}

    partner = at(x, z, 1 - core)
    peers = [partner]
    peers += [along_x(step) for step in range(1, X_CHIPS)]
    peers += [along_z(step) for step in range(1, Z_CHIPS)]
    peers += [along_y(step) for step in range(1, Y_CHIPS)]
    barrier = pltpu.get_barrier_semaphore()
    for peer in peers:
        pl.semaphore_signal(barrier, inc=1, device_id=peer, device_id_type=MESH)
    pl.semaphore_wait(barrier, len(peers))

    def send(src, dst, send_sem, recv_sem, peer):
        copy = pltpu.make_async_remote_copy(
            src_ref=src, dst_ref=dst, send_sem=send_sem, recv_sem=recv_sem, device_id=peer, device_id_type=MESH
        )
        copy.start()
        return copy

    def finish(copies):
        for copy in copies:
            copy.wait()

    other_lanes = pl.ds(pl.multiple_of((1 - core) * half, half), half)
    own_lanes = pl.ds(pl.multiple_of(core * half, half), half)
    finish([send(mine_ref.at[:, other_lanes], from_core, core_send, core_recv, partner)])
    held[...] = mine_ref[:, own_lanes] + from_core[...]

    copies = []
    for step in range(1, X_CHIPS):
        to = pl.multiple_of(lax.rem(x + step, X_CHIPS) * x_rows, x_rows)
        copies.append(
            send(held.at[pl.ds(to, x_rows), :], from_x.at[step], x_send.at[step], x_recv.at[step], along_x(step))
        )
    finish(copies)
    total = held[pl.ds(pl.multiple_of(x * x_rows, x_rows), x_rows), :]
    for step in range(1, X_CHIPS):
        total = total + from_x[step]
    from_x[0] = total

    copies = []
    for step in range(1, Z_CHIPS):
        to = pl.multiple_of(lax.rem(z + step, Z_CHIPS) * z_rows, z_rows)
        copies.append(
            send(from_x.at[0, pl.ds(to, z_rows), :], from_z.at[step], z_send.at[step], z_recv.at[step], along_z(step))
        )
    finish(copies)
    own = pl.ds(pl.multiple_of(z * z_rows, z_rows), z_rows)
    total = from_x[0, own, :]
    for step in range(1, Z_CHIPS):
        total = total + from_z[step]
    out_ref[core, y, x, own, :] = total

    piece = out_ref.at[core, y, x, own, :]
    finish(
        [send(piece, piece, gz_send.at[step], gz_recv.at[step], along_z(step)) for step in range(1, Z_CHIPS)]
    )
    low, high = pl.ds(0, split), pl.ds(split, split)
    copies = []
    piece = out_ref.at[core, y, x, low, :]
    for step in range(1, X_CHIPS):
        copies.append(send(piece, piece, ga_send.at[0, step], ga_recv.at[0, step], along_x(step)))
    piece = out_ref.at[core, y, x, high, :]
    for step in range(1, Y_CHIPS):
        copies.append(send(piece, piece, ga_send.at[1, step], ga_recv.at[1, step], along_y(step)))
    finish(copies)
    copies = []
    piece = out_ref.at[core, y, :, low, :]
    for step in range(1, Y_CHIPS):
        copies.append(send(piece, piece, gb_send.at[0, step], gb_recv.at[0, step], along_y(step)))
    piece = out_ref.at[core, :, x, high, :]
    for step in range(1, X_CHIPS):
        copies.append(send(piece, piece, gb_send.at[1, step], gb_recv.at[1, step], along_x(step)))
    finish(copies)
    piece = out_ref.at[core]
    finish([send(piece, piece, gc_send, gc_recv, partner)])


def total_moments(packed):
    rows, width = packed.shape
    half, x_rows = width // CORES, rows // X_CHIPS
    vmem = pl.BlockSpec(memory_space=pltpu.VMEM)
    dma = pltpu.SemaphoreType.DMA
    out = pl.pallas_call(
        total_kernel,
        out_shape=jax.ShapeDtypeStruct((CORES, Y_CHIPS, X_CHIPS, x_rows, half), jnp.float32),
        in_specs=[vmem],
        out_specs=vmem,
        scratch_shapes=[
            pltpu.VMEM((rows, half), jnp.float32),
            pltpu.VMEM((rows, half), jnp.float32),
            pltpu.VMEM((X_CHIPS, x_rows, half), jnp.float32),
            pltpu.VMEM((Z_CHIPS, x_rows // Z_CHIPS, half), jnp.float32),
            dma,
            dma,
            dma((X_CHIPS,)),
            dma((X_CHIPS,)),
            dma((Z_CHIPS,)),
            dma((Z_CHIPS,)),
            dma((Z_CHIPS,)),
            dma((Z_CHIPS,)),
            dma((2, X_CHIPS)),
            dma((2, X_CHIPS)),
            dma((2, X_CHIPS)),
            dma((2, X_CHIPS)),
            dma,
            dma,
        ],
        compiler_params=pltpu.CompilerParams(collective_id=0, has_side_effects=True),
        name="total_moments",
    )(packed)
    return out.reshape(CORES, Y_CHIPS * rows, half)


def shards(features, seg_lengths):
    frame_rows = features.shape[0]
    feat_width = features.shape[1]
    feat_count = lax.axis_size("feat")
    tm_index = lax.axis_index("tm")
    feat_index = lax.axis_index("feat")
    col_block = feat_width // feat_count
    comp_block = NC // feat_count
    tail_part = from_behind(features[:LAG], "tm", -1)
    ahead_rows = jnp.concatenate([features[LAG:], tail_part], axis=0)
    seg_ends = jnp.cumsum(seg_lengths).astype(jnp.int32)
    moments = tm_index * frame_rows - LAG + jnp.arange(frame_rows + LAG, dtype=jnp.int32)
    inside = (seg_ends[:, None] > moments[None, :]) & (seg_ends[:, None] <= moments[None, :] + LAG)
    clear = jnp.logical_not(jnp.any(inside, axis=0)) & (moments >= 0)
    valid_wide = clear.astype(jnp.float32)
    validity = valid_wide[LAG:]
    uses = (validity + valid_wide[:frame_rows]).astype(jnp.bfloat16)
    start_col = feat_index * col_block
    lead_cols = lax.dynamic_slice_in_dim(features, start_col, col_block, 1)
    gram_rows = contract(lead_cols * uses[:, None], features)
    cross_rows = contract(lead_cols * validity.astype(jnp.bfloat16)[:, None], ahead_rows)
    sums = jnp.dot(uses, features, preferred_element_type=jnp.float32)
    sum_rows = jnp.pad(sums.reshape(feat_count, col_block), ((0, 8 - feat_count), (0, 0)))
    before = lax.rem(feat_index + feat_count - 1, feat_count) * col_block
    gram_rows = lax.dynamic_update_slice(gram_rows, sum_rows, (0, before))
    gathered = total_moments(jnp.concatenate([gram_rows, cross_rows], axis=0))
    koopman_rows, first_part, second_part, offset = whiten(
        feat_index.astype(jnp.int32).reshape(1),
        seg_lengths.reshape(1, -1),
        gathered,
        col_block,
        comp_block,
    )
    forward = jnp.einsum("cf,tf->ct", first_part, ahead_rows, preferred_element_type=jnp.float32)
    backward = jnp.einsum("cf,tf->ct", second_part, features, preferred_element_type=jnp.float32)
    lag_error = (forward - backward - offset[:, :1]) * validity[None, :]
    return (koopman_rows, lag_error)


def solution(mesh):
    in_specs = (P("tm", None), P())
    out_specs = (P("feat", None), P("feat", "tm"))
    return jax.shard_map(shards, mesh=mesh, in_specs=in_specs, out_specs=out_specs, check_vma=False)
```

```python
import jax
import jax.numpy as jnp
from jax import lax
from jax.experimental import pallas as pl
from jax.experimental.pallas import tpu as pltpu
from jax.sharding import PartitionSpec as P

LAG = 64
NC = 128

RIDGE = 0.05
HIGHEST = lax.Precision.HIGHEST
LEAF = 128
MESH = pl.DeviceIdType.MESH
X_CHIPS, Y_CHIPS, Z_CHIPS, CORES = 4, 4, 8, 2


def from_behind(shard, axis, by):
    count = lax.axis_size(axis)
    pairs = [(i, i + by) for i in range(count) if 0 <= i + by < count]
    return lax.ppermute(shard, axis, pairs)


def contract(left_rows, right_rows):
    return lax.dot_general(
        left_rows, right_rows, (((0,), (0,)), ((), ())), preferred_element_type=jnp.float32
    )


def exact_dot(left, right, left_dim=1, right_dim=0):
    return lax.dot_general(
        left,
        right,
        (((left_dim,), (right_dim,)), ((), ())),
        precision=HIGHEST,
        preferred_element_type=jnp.float32,
    )


def leaf_inverse(square):
    count = LEAF // 8
    tiles = [square[8 * i : 8 * i + 8, :] for i in range(count)]
    lanes = lax.broadcasted_iota(jnp.int32, (8, LEAF), 1)
    subs = lax.broadcasted_iota(jnp.int32, (8, LEAF), 0)

    def spread(tile, sub):
        return jnp.broadcast_to(tile[sub : sub + 1, :], (8, LEAF))

    for g in range(count):
        first = 8 * g
        own = tiles[g]
        columns = [jnp.broadcast_to(own[:, first + k : first + k + 1], (8, LEAF)) for k in range(8)]
        in_block = (lanes >= first) & (lanes < first + 8)
        rows = jnp.where(in_block, jnp.where(lanes - first == subs, 1.0, 0.0), own)
        pivots = columns[0]
        if g + 1 < count:
            after = tiles[g + 1]
            after_columns = [
                jnp.broadcast_to(after[:, first + k : first + k + 1], (8, LEAF)) for k in range(8)
            ]
            after = jnp.where(in_block, 0.0, after)
        for k in range(8):
            corner_rows = [spread(columns[m], k) for m in range(k, 8)]
            row = spread(rows, k)
            flip = 1.0 / corner_rows[0]
            pivots = jnp.where(subs == k, columns[k], pivots)
            factor = jnp.where(subs > k, columns[k] * flip, 0.0)
            rows = rows - factor * row
            for m in range(k + 1, 8):
                columns[m] = columns[m] - factor * corner_rows[m - k]
            if g + 1 < count:
                factor = after_columns[k] * flip
                after = after - factor * row
                for m in range(k + 1, 8):
                    after_columns[m] = after_columns[m] - factor * corner_rows[m - k]
        rows = rows * lax.rsqrt(pivots)
        tiles[g] = rows
        if g + 1 < count:
            tiles[g + 1] = after
        if g + 2 < count:
            turned = rows.T
            spreads = [spread(rows, k) for k in range(8)]
            for i in range(g + 2, count):
                tile = jnp.where(in_block, 0.0, tiles[i])
                for k in range(8):
                    tile = tile - jnp.broadcast_to(turned[8 * i : 8 * i + 8, k : k + 1], (8, LEAF)) * spreads[k]
                tiles[i] = tile
    outs = [jnp.where(lanes <= subs + 8 * i, tiles[i], 0.0) for i in range(count)]
    return jnp.concatenate(outs, axis=0)


def whiten_kernel(
    index_ref, lengths_ref, moments_ref, koop_ref, first_ref, second_ref, offset_ref, work, cov
):
    feat_width = work.shape[0]
    blocks = feat_width // LEAF
    part = koop_ref.shape[0]
    pairs = jnp.maximum(lengths_ref[...] - LAG, 0).astype(jnp.float32)
    scale = 1.0 / (2.0 * jnp.sum(pairs, axis=1, keepdims=True))

    def moment(kind, k, m):
        top, left = LEAF * (2 * k + kind), LEAF * (m % 2)
        return moments_ref[m // 2, top : top + LEAF, left : left + LEAF]

    def gram_block(k, m):
        return moment(0, m, k).T if m == (k + blocks - 1) % blocks else moment(0, k, m)

    sums = moment(0, 0, blocks - 1)
    mean = jnp.concatenate([sums[m : m + 1, :] for m in range(blocks)], axis=1) * scale
    mean_cols = jnp.broadcast_to(mean, (LEAF, feat_width)).T
    rows_io = lax.broadcasted_iota(jnp.int32, (LEAF, LEAF), 0)
    lanes_io = lax.broadcasted_iota(jnp.int32, (LEAF, LEAF), 1)
    eye = rows_io == lanes_io
    trace = jnp.zeros((1, 1), jnp.float32)
    for k in range(blocks):
        square = gram_block(k, k) * scale - mean_cols[LEAF * k : LEAF * k + LEAF, :] * mean[:, LEAF * k : LEAF * k + LEAF]
        diag = jnp.sum(jnp.where(eye, square, 0.0), axis=0, keepdims=True)
        trace = trace + jnp.sum(diag, axis=1, keepdims=True)
    ridge = RIDGE * (trace / feat_width)
    for k in range(blocks):
        for m in range(blocks):
            outer = mean_cols[LEAF * k : LEAF * k + LEAF, :] * mean[:, LEAF * m : LEAF * m + LEAF]
            block = gram_block(k, m) * scale - outer
            if k == m:
                block = block + jnp.where(eye, ridge, 0.0)
            work[LEAF * k : LEAF * k + LEAF, LEAF * m : LEAF * m + LEAF] = block
            straight = moment(1, k, m)
            turned = moment(1, m, k).T
            cov[LEAF * k : LEAF * k + LEAF, LEAF * m : LEAF * m + LEAF] = (straight + turned) * scale - outer

    def eliminate(k, carry):
        start = pl.multiple_of(k * LEAF, LEAF)
        inverse = leaf_inverse(work[pl.ds(start, LEAF), pl.ds(start, LEAF)])
        work[pl.ds(start, LEAF), pl.ds(start, LEAF)] = jnp.where(eye, 1.0, 0.0)
        panel = exact_dot(inverse, work[pl.ds(start, LEAF), :])
        wide_lanes = lax.broadcasted_iota(jnp.int32, (LEAF, feat_width), 1)
        in_block = (wide_lanes >= start) & (wide_lanes < start + LEAF)
        for i in range(1, blocks):

            @pl.when(k < i)
            def _(i=i):
                old = jnp.where(in_block, 0.0, work[LEAF * i : LEAF * i + LEAF, :])
                change = exact_dot(panel[:, LEAF * i : LEAF * i + LEAF], panel, 0, 0)
                work[LEAF * i : LEAF * i + LEAF, :] = old - change

        work[pl.ds(start, LEAF), :] = panel
        return carry

    lax.fori_loop(0, blocks, eliminate, 0)
    rows_io = lax.broadcasted_iota(jnp.int32, (feat_width, feat_width), 0)
    lanes_io = lax.broadcasted_iota(jnp.int32, (feat_width, feat_width), 1)
    work[...] = jnp.where(rows_io >= lanes_io, work[...], 0.0)
    index = index_ref[0]
    comps = first_ref.shape[0]
    own_rows = work[pl.ds(pl.multiple_of(index * part, part), part), :]
    own_comps = work[pl.ds(pl.multiple_of(index * comps, comps), comps), :]
    stacked = jnp.concatenate([own_rows, own_comps], axis=0)
    koop = exact_dot(exact_dot(stacked, cov[...]), work[...], 1, 1)
    koop_ref[...] = koop[:part, :]
    first = own_comps.astype(jnp.bfloat16)
    second = exact_dot(koop[part:, :], work[...]).astype(jnp.bfloat16)
    first_ref[...] = first
    second_ref[...] = second
    gap = (first.astype(jnp.float32) - second.astype(jnp.float32)) * mean
    offset_ref[...] = jnp.broadcast_to(jnp.sum(gap, axis=1, keepdims=True), offset_ref.shape)


def whiten(index, lengths, moments, part, comps):
    feat_width = 2 * moments.shape[2]
    vmem = pl.BlockSpec(memory_space=pltpu.VMEM)
    return pl.pallas_call(
        whiten_kernel,
        out_shape=(
            jax.ShapeDtypeStruct((part, feat_width), jnp.float32),
            jax.ShapeDtypeStruct((comps, feat_width), jnp.bfloat16),
            jax.ShapeDtypeStruct((comps, feat_width), jnp.bfloat16),
            jax.ShapeDtypeStruct((comps, 128), jnp.float32),
        ),
        in_specs=[pl.BlockSpec(memory_space=pltpu.SMEM), vmem, vmem],
        out_specs=(vmem, vmem, vmem, vmem),
        scratch_shapes=[
            pltpu.VMEM((feat_width, feat_width), jnp.float32),
            pltpu.VMEM((feat_width, feat_width), jnp.float32),
        ],
        name="whiten",
    )(index, lengths, moments)


def total_kernel(
    mine_ref, out_ref, from_core, held, from_x, from_z, core_send, core_recv, x_send, x_recv, z_send, z_recv,
    gz_send, gz_recv, ga_send, ga_recv, gb_send, gb_recv, gc_send, gc_recv
):
    place, y = lax.axis_index("tm"), lax.axis_index("feat")
    core = lax.rem(place, CORES)
    z = lax.rem(lax.div(place, CORES), Z_CHIPS)
    x = lax.div(place, CORES * Z_CHIPS)
    rows, half = held.shape
    x_rows = rows // X_CHIPS
    z_rows = x_rows // Z_CHIPS
    split = x_rows // 2

    def at(x_to, z_to, core_to):
        return {"tm": (x_to * Z_CHIPS + z_to) * CORES + core_to}

    def along_x(step):
        return at(lax.rem(x + step, X_CHIPS), z, core)

    def along_z(step):
        return at(x, lax.rem(z + step, Z_CHIPS), core)

    def along_y(step):
        return {"feat": lax.rem(y + step, Y_CHIPS)}

    partner = at(x, z, 1 - core)
    peers = [partner]
    peers += [along_x(step) for step in range(1, X_CHIPS)]
    peers += [along_z(step) for step in range(1, Z_CHIPS)]
    peers += [along_y(step) for step in range(1, Y_CHIPS)]
    barrier = pltpu.get_barrier_semaphore()
    for peer in peers:
        pl.semaphore_signal(barrier, inc=1, device_id=peer, device_id_type=MESH)
    pl.semaphore_wait(barrier, len(peers))

    def send(src, dst, send_sem, recv_sem, peer):
        copy = pltpu.make_async_remote_copy(
            src_ref=src, dst_ref=dst, send_sem=send_sem, recv_sem=recv_sem, device_id=peer, device_id_type=MESH
        )
        copy.start()
        return copy

    def finish(copies):
        for copy in copies:
            copy.wait()

    other_lanes = pl.ds(pl.multiple_of((1 - core) * half, half), half)
    own_lanes = pl.ds(pl.multiple_of(core * half, half), half)
    finish([send(mine_ref.at[:, other_lanes], from_core, core_send, core_recv, partner)])
    held[...] = mine_ref[:, own_lanes] + from_core[...]

    copies = []
    for step in range(1, X_CHIPS):
        to = pl.multiple_of(lax.rem(x + step, X_CHIPS) * x_rows, x_rows)
        copies.append(
            send(held.at[pl.ds(to, x_rows), :], from_x.at[step], x_send.at[step], x_recv.at[step], along_x(step))
        )
    finish(copies)
    total = held[pl.ds(pl.multiple_of(x * x_rows, x_rows), x_rows), :]
    for step in range(1, X_CHIPS):
        total = total + from_x[step]
    from_x[0] = total

    copies = []
    for step in range(1, Z_CHIPS):
        to = pl.multiple_of(lax.rem(z + step, Z_CHIPS) * z_rows, z_rows)
        copies.append(
            send(from_x.at[0, pl.ds(to, z_rows), :], from_z.at[step], z_send.at[step], z_recv.at[step], along_z(step))
        )
    finish(copies)
    own = pl.ds(pl.multiple_of(z * z_rows, z_rows), z_rows)
    total = from_x[0, own, :]
    for step in range(1, Z_CHIPS):
        total = total + from_z[step]
    out_ref[core, y, x, own, :] = total

    piece = out_ref.at[core, y, x, own, :]
    finish(
        [send(piece, piece, gz_send.at[step], gz_recv.at[step], along_z(step)) for step in range(1, Z_CHIPS)]
    )
    low, high = pl.ds(0, split), pl.ds(split, split)
    copies = []
    piece = out_ref.at[core, y, x, low, :]
    for step in range(1, X_CHIPS):
        copies.append(send(piece, piece, ga_send.at[0, step], ga_recv.at[0, step], along_x(step)))
    piece = out_ref.at[core, y, x, high, :]
    for step in range(1, Y_CHIPS):
        copies.append(send(piece, piece, ga_send.at[1, step], ga_recv.at[1, step], along_y(step)))
    finish(copies)
    copies = []
    piece = out_ref.at[core, y, :, low, :]
    for step in range(1, Y_CHIPS):
        copies.append(send(piece, piece, gb_send.at[0, step], gb_recv.at[0, step], along_y(step)))
    piece = out_ref.at[core, :, x, high, :]
    for step in range(1, X_CHIPS):
        copies.append(send(piece, piece, gb_send.at[1, step], gb_recv.at[1, step], along_x(step)))
    finish(copies)
    piece = out_ref.at[core]
    finish([send(piece, piece, gc_send, gc_recv, partner)])


def total_moments(packed):
    rows, width = packed.shape
    half, x_rows = width // CORES, rows // X_CHIPS
    vmem = pl.BlockSpec(memory_space=pltpu.VMEM)
    dma = pltpu.SemaphoreType.DMA
    out = pl.pallas_call(
        total_kernel,
        out_shape=jax.ShapeDtypeStruct((CORES, Y_CHIPS, X_CHIPS, x_rows, half), jnp.float32),
        in_specs=[vmem],
        out_specs=vmem,
        scratch_shapes=[
            pltpu.VMEM((rows, half), jnp.float32),
            pltpu.VMEM((rows, half), jnp.float32),
            pltpu.VMEM((X_CHIPS, x_rows, half), jnp.float32),
            pltpu.VMEM((Z_CHIPS, x_rows // Z_CHIPS, half), jnp.float32),
            dma,
            dma,
            dma((X_CHIPS,)),
            dma((X_CHIPS,)),
            dma((Z_CHIPS,)),
            dma((Z_CHIPS,)),
            dma((Z_CHIPS,)),
            dma((Z_CHIPS,)),
            dma((2, X_CHIPS)),
            dma((2, X_CHIPS)),
            dma((2, X_CHIPS)),
            dma((2, X_CHIPS)),
            dma,
            dma,
        ],
        compiler_params=pltpu.CompilerParams(collective_id=0, has_side_effects=True),
        name="total_moments",
    )(packed)
    return out.reshape(CORES, Y_CHIPS * rows, half)


def shards(features, seg_lengths):
    frame_rows = features.shape[0]
    feat_width = features.shape[1]
    feat_count = lax.axis_size("feat")
    tm_index = lax.axis_index("tm")
    feat_index = lax.axis_index("feat")
    col_block = feat_width // feat_count
    comp_block = NC // feat_count
    tail_part = from_behind(features[:LAG], "tm", -1)
    ahead_rows = jnp.concatenate([features[LAG:], tail_part], axis=0)
    seg_ends = jnp.cumsum(seg_lengths).astype(jnp.int32)
    moments = tm_index * frame_rows - LAG + jnp.arange(frame_rows + LAG, dtype=jnp.int32)
    inside = (seg_ends[:, None] > moments[None, :]) & (seg_ends[:, None] <= moments[None, :] + LAG)
    clear = jnp.logical_not(jnp.any(inside, axis=0)) & (moments >= 0)
    valid_wide = clear.astype(jnp.float32)
    validity = valid_wide[LAG:]
    uses = (validity + valid_wide[:frame_rows]).astype(jnp.bfloat16)
    start_col = feat_index * col_block
    lead_cols = lax.dynamic_slice_in_dim(features, start_col, col_block, 1)
    gram_rows = contract(lead_cols * uses[:, None], features)
    cross_rows = contract(lead_cols * validity.astype(jnp.bfloat16)[:, None], ahead_rows)
    sums = jnp.dot(uses, features, preferred_element_type=jnp.float32)
    sum_rows = jnp.pad(sums.reshape(feat_count, col_block), ((0, 8 - feat_count), (0, 0)))
    before = lax.rem(feat_index + feat_count - 1, feat_count) * col_block
    gram_rows = lax.dynamic_update_slice(gram_rows, sum_rows, (0, before))
    gathered = total_moments(jnp.concatenate([gram_rows, cross_rows], axis=0))
    koopman_rows, first_part, second_part, offset = whiten(
        feat_index.astype(jnp.int32).reshape(1),
        seg_lengths.reshape(1, -1),
        gathered,
        col_block,
        comp_block,
    )
    forward = jnp.einsum("cf,tf->ct", first_part, ahead_rows, preferred_element_type=jnp.float32)
    backward = jnp.einsum("cf,tf->ct", second_part, features, preferred_element_type=jnp.float32)
    lag_error = (forward - backward - offset[:, :1]) * validity[None, :]
    return (koopman_rows, lag_error)


def solution(mesh):
    in_specs = (P("tm", None), P())
    out_specs = (P("feat", None), P("feat", "tm"))
    return jax.shard_map(shards, mesh=mesh, in_specs=in_specs, out_specs=out_specs, check_vma=False)
```

```python
import jax
import jax.numpy as jnp
from jax import lax
from jax.experimental import pallas as pl
from jax.experimental.pallas import tpu as pltpu
from jax.sharding import PartitionSpec as P

LAG = 64
NC = 128

RIDGE = 0.05
HIGHEST = lax.Precision.HIGHEST
LEAF = 128
MESH = pl.DeviceIdType.MESH
X_CHIPS, Y_CHIPS, Z_CHIPS, CORES = 4, 4, 8, 2


def from_behind(shard, axis, by):
    count = lax.axis_size(axis)
    pairs = [(i, i + by) for i in range(count) if 0 <= i + by < count]
    return lax.ppermute(shard, axis, pairs)


def contract(left_rows, right_rows):
    return lax.dot_general(
        left_rows, right_rows, (((0,), (0,)), ((), ())), preferred_element_type=jnp.float32
    )


def exact_dot(left, right, left_dim=1, right_dim=0):
    return lax.dot_general(
        left,
        right,
        (((left_dim,), (right_dim,)), ((), ())),
        precision=HIGHEST,
        preferred_element_type=jnp.float32,
    )


def leaf_inverse(square):
    count = LEAF // 8
    tiles = [square[8 * i : 8 * i + 8, :] for i in range(count)]
    lanes = lax.broadcasted_iota(jnp.int32, (8, LEAF), 1)
    subs = lax.broadcasted_iota(jnp.int32, (8, LEAF), 0)

    def spread(tile, sub):
        return jnp.broadcast_to(tile[sub : sub + 1, :], (8, LEAF))

    for g in range(count):
        first = 8 * g
        own = tiles[g]
        columns = [jnp.broadcast_to(own[:, first + k : first + k + 1], (8, LEAF)) for k in range(8)]
        in_block = (lanes >= first) & (lanes < first + 8)
        rows = jnp.where(in_block, jnp.where(lanes - first == subs, 1.0, 0.0), own)
        pivots = columns[0]
        if g + 1 < count:
            after = tiles[g + 1]
            after_columns = [
                jnp.broadcast_to(after[:, first + k : first + k + 1], (8, LEAF)) for k in range(8)
            ]
            after = jnp.where(in_block, 0.0, after)
        for k in range(8):
            corner_rows = [spread(columns[m], k) for m in range(k, 8)]
            row = spread(rows, k)
            flip = 1.0 / corner_rows[0]
            pivots = jnp.where(subs == k, columns[k], pivots)
            factor = jnp.where(subs > k, columns[k] * flip, 0.0)
            rows = rows - factor * row
            for m in range(k + 1, 8):
                columns[m] = columns[m] - factor * corner_rows[m - k]
            if g + 1 < count:
                factor = after_columns[k] * flip
                after = after - factor * row
                for m in range(k + 1, 8):
                    after_columns[m] = after_columns[m] - factor * corner_rows[m - k]
        rows = rows * lax.rsqrt(pivots)
        tiles[g] = rows
        if g + 1 < count:
            tiles[g + 1] = after
        if g + 2 < count:
            turned = rows.T
            spreads = [spread(rows, k) for k in range(8)]
            for i in range(g + 2, count):
                tile = jnp.where(in_block, 0.0, tiles[i])
                for k in range(8):
                    tile = tile - jnp.broadcast_to(turned[8 * i : 8 * i + 8, k : k + 1], (8, LEAF)) * spreads[k]
                tiles[i] = tile
    outs = [jnp.where(lanes <= subs + 8 * i, tiles[i], 0.0) for i in range(count)]
    return jnp.concatenate(outs, axis=0)


def whiten_kernel(
    index_ref, lengths_ref, moments_ref, koop_ref, first_ref, second_ref, offset_ref, work, cov
):
    feat_width = work.shape[0]
    blocks = feat_width // LEAF
    part = koop_ref.shape[0]
    pairs = jnp.maximum(lengths_ref[...] - LAG, 0).astype(jnp.float32)
    scale = 1.0 / (2.0 * jnp.sum(pairs, axis=1, keepdims=True))

    def moment(kind, k, m):
        top, left = LEAF * (2 * k + kind), LEAF * (m % 2)
        return moments_ref[m // 2, top : top + LEAF, left : left + LEAF]

    def gram_block(k, m):
        return moment(0, m, k).T if m == (k + blocks - 1) % blocks else moment(0, k, m)

    sums = moment(0, 0, blocks - 1)
    mean = jnp.concatenate([sums[m : m + 1, :] for m in range(blocks)], axis=1) * scale
    mean_cols = jnp.broadcast_to(mean, (LEAF, feat_width)).T
    rows_io = lax.broadcasted_iota(jnp.int32, (LEAF, LEAF), 0)
    lanes_io = lax.broadcasted_iota(jnp.int32, (LEAF, LEAF), 1)
    eye = rows_io == lanes_io
    trace = jnp.zeros((1, 1), jnp.float32)
    for k in range(blocks):
        square = gram_block(k, k) * scale - mean_cols[LEAF * k : LEAF * k + LEAF, :] * mean[:, LEAF * k : LEAF * k + LEAF]
        diag = jnp.sum(jnp.where(eye, square, 0.0), axis=0, keepdims=True)
        trace = trace + jnp.sum(diag, axis=1, keepdims=True)
    ridge = RIDGE * (trace / feat_width)
    for k in range(blocks):
        for m in range(blocks):
            outer = mean_cols[LEAF * k : LEAF * k + LEAF, :] * mean[:, LEAF * m : LEAF * m + LEAF]
            block = gram_block(k, m) * scale - outer
            if k == m:
                block = block + jnp.where(eye, ridge, 0.0)
            work[LEAF * k : LEAF * k + LEAF, LEAF * m : LEAF * m + LEAF] = block
            straight = moment(1, k, m)
            turned = moment(1, m, k).T
            cov[LEAF * k : LEAF * k + LEAF, LEAF * m : LEAF * m + LEAF] = (straight + turned) * scale - outer

    def eliminate(k, carry):
        start = pl.multiple_of(k * LEAF, LEAF)
        inverse = leaf_inverse(work[pl.ds(start, LEAF), pl.ds(start, LEAF)])
        work[pl.ds(start, LEAF), pl.ds(start, LEAF)] = jnp.where(eye, 1.0, 0.0)
        panel = exact_dot(inverse, work[pl.ds(start, LEAF), :])
        wide_lanes = lax.broadcasted_iota(jnp.int32, (LEAF, feat_width), 1)
        in_block = (wide_lanes >= start) & (wide_lanes < start + LEAF)
        for i in range(1, blocks):

            @pl.when(k < i)
            def _(i=i):
                old = jnp.where(in_block, 0.0, work[LEAF * i : LEAF * i + LEAF, :])
                change = exact_dot(panel[:, LEAF * i : LEAF * i + LEAF], panel, 0, 0)
                work[LEAF * i : LEAF * i + LEAF, :] = old - change

        work[pl.ds(start, LEAF), :] = panel
        return carry

    lax.fori_loop(0, blocks, eliminate, 0)
    rows_io = lax.broadcasted_iota(jnp.int32, (feat_width, feat_width), 0)
    lanes_io = lax.broadcasted_iota(jnp.int32, (feat_width, feat_width), 1)
    work[...] = jnp.where(rows_io >= lanes_io, work[...], 0.0)
    index = index_ref[0]
    comps = first_ref.shape[0]
    own_rows = work[pl.ds(pl.multiple_of(index * part, part), part), :]
    own_comps = work[pl.ds(pl.multiple_of(index * comps, comps), comps), :]
    stacked = jnp.concatenate([own_rows, own_comps], axis=0)
    koop = exact_dot(exact_dot(stacked, cov[...]), work[...], 1, 1)
    koop_ref[...] = koop[:part, :]
    first = own_comps.astype(jnp.bfloat16)
    second = exact_dot(koop[part:, :], work[...]).astype(jnp.bfloat16)
    first_ref[...] = first
    second_ref[...] = second
    gap = (first.astype(jnp.float32) - second.astype(jnp.float32)) * mean
    offset_ref[...] = jnp.broadcast_to(jnp.sum(gap, axis=1, keepdims=True), offset_ref.shape)


def whiten(index, lengths, moments, part, comps):
    feat_width = 2 * moments.shape[2]
    vmem = pl.BlockSpec(memory_space=pltpu.VMEM)
    return pl.pallas_call(
        whiten_kernel,
        out_shape=(
            jax.ShapeDtypeStruct((part, feat_width), jnp.float32),
            jax.ShapeDtypeStruct((comps, feat_width), jnp.bfloat16),
            jax.ShapeDtypeStruct((comps, feat_width), jnp.bfloat16),
            jax.ShapeDtypeStruct((comps, 128), jnp.float32),
        ),
        in_specs=[pl.BlockSpec(memory_space=pltpu.SMEM), vmem, vmem],
        out_specs=(vmem, vmem, vmem, vmem),
        scratch_shapes=[
            pltpu.VMEM((feat_width, feat_width), jnp.float32),
            pltpu.VMEM((feat_width, feat_width), jnp.float32),
        ],
        name="whiten",
    )(index, lengths, moments)


def total_kernel(
    mine_ref, out_ref, from_core, held, from_x, from_z, core_send, core_recv, x_send, x_recv, z_send, z_recv,
    gz_send, gz_recv, ga_send, ga_recv, gb_send, gb_recv, gc_send, gc_recv
):
    place, y = lax.axis_index("tm"), lax.axis_index("feat")
    core = lax.rem(place, CORES)
    z = lax.rem(lax.div(place, CORES), Z_CHIPS)
    x = lax.div(place, CORES * Z_CHIPS)
    rows, half = held.shape
    x_rows = rows // X_CHIPS
    z_rows = x_rows // Z_CHIPS
    split = x_rows // 2

    def at(x_to, z_to, core_to):
        return {"tm": (x_to * Z_CHIPS + z_to) * CORES + core_to}

    def along_x(step):
        return at(lax.rem(x + step, X_CHIPS), z, core)

    def along_z(step):
        return at(x, lax.rem(z + step, Z_CHIPS), core)

    def along_y(step):
        return {"feat": lax.rem(y + step, Y_CHIPS)}

    partner = at(x, z, 1 - core)
    peers = [partner]
    peers += [along_x(step) for step in range(1, X_CHIPS)]
    peers += [along_z(step) for step in range(1, Z_CHIPS)]
    peers += [along_y(step) for step in range(1, Y_CHIPS)]
    barrier = pltpu.get_barrier_semaphore()
    for peer in peers:
        pl.semaphore_signal(barrier, inc=1, device_id=peer, device_id_type=MESH)
    pl.semaphore_wait(barrier, len(peers))

    def send(src, dst, send_sem, recv_sem, peer):
        copy = pltpu.make_async_remote_copy(
            src_ref=src, dst_ref=dst, send_sem=send_sem, recv_sem=recv_sem, device_id=peer, device_id_type=MESH
        )
        copy.start()
        return copy

    def finish(copies):
        for copy in copies:
            copy.wait()

    other_lanes = pl.ds(pl.multiple_of((1 - core) * half, half), half)
    own_lanes = pl.ds(pl.multiple_of(core * half, half), half)
    finish([send(mine_ref.at[:, other_lanes], from_core, core_send, core_recv, partner)])
    held[...] = mine_ref[:, own_lanes] + from_core[...]

    copies = []
    for step in range(1, X_CHIPS):
        to = pl.multiple_of(lax.rem(x + step, X_CHIPS) * x_rows, x_rows)
        copies.append(
            send(held.at[pl.ds(to, x_rows), :], from_x.at[step], x_send.at[step], x_recv.at[step], along_x(step))
        )
    finish(copies)
    total = held[pl.ds(pl.multiple_of(x * x_rows, x_rows), x_rows), :]
    for step in range(1, X_CHIPS):
        total = total + from_x[step]
    from_x[0] = total

    copies = []
    for step in range(1, Z_CHIPS):
        to = pl.multiple_of(lax.rem(z + step, Z_CHIPS) * z_rows, z_rows)
        copies.append(
            send(from_x.at[0, pl.ds(to, z_rows), :], from_z.at[step], z_send.at[step], z_recv.at[step], along_z(step))
        )
    finish(copies)
    own = pl.ds(pl.multiple_of(z * z_rows, z_rows), z_rows)
    total = from_x[0, own, :]
    for step in range(1, Z_CHIPS):
        total = total + from_z[step]
    out_ref[core, y, x, own, :] = total

    piece = out_ref.at[core, y, x, own, :]
    finish(
        [send(piece, piece, gz_send.at[step], gz_recv.at[step], along_z(step)) for step in range(1, Z_CHIPS)]
    )
    low, high = pl.ds(0, split), pl.ds(split, split)
    forwarded = []

    def forward(piece):
        slot = len(forwarded)
        forwarded.append(send(piece, piece, gc_send.at[slot], gc_recv.at[slot], partner))

    def back(place, step, count):
        return lax.rem(place + count - step, count)

    first_x, first_y, next_x, next_y = [], [], [], []
    piece = out_ref.at[core, y, x, low, :]
    for step in range(1, X_CHIPS):
        first_x.append(send(piece, piece, ga_send.at[0, step], ga_recv.at[0, step], along_x(step)))
    piece = out_ref.at[core, y, x, high, :]
    for step in range(1, Y_CHIPS):
        first_y.append(send(piece, piece, ga_send.at[1, step], ga_recv.at[1, step], along_y(step)))
    forward(out_ref.at[core, y, x])
    finish(first_x)
    piece = out_ref.at[core, y, :, low, :]
    for step in range(1, Y_CHIPS):
        next_y.append(send(piece, piece, gb_send.at[0, step], gb_recv.at[0, step], along_y(step)))
    finish(first_y)
    piece = out_ref.at[core, :, x, high, :]
    for step in range(1, X_CHIPS):
        next_x.append(send(piece, piece, gb_send.at[1, step], gb_recv.at[1, step], along_x(step)))
    for step in range(1, X_CHIPS):
        forward(out_ref.at[core, y, back(x, step, X_CHIPS), low, :])
    for step in range(1, Y_CHIPS):
        forward(out_ref.at[core, back(y, step, Y_CHIPS), x, high, :])
    for step in (1, 3, 2):
        next_y[step - 1].wait()
        forward(out_ref.at[core, back(y, step, Y_CHIPS), :, low, :])
        next_x[step - 1].wait()
        forward(out_ref.at[core, :, back(x, step, X_CHIPS), high, :])
    finish(forwarded)


def total_moments(packed):
    rows, width = packed.shape
    half, x_rows = width // CORES, rows // X_CHIPS
    vmem = pl.BlockSpec(memory_space=pltpu.VMEM)
    dma = pltpu.SemaphoreType.DMA
    out = pl.pallas_call(
        total_kernel,
        out_shape=jax.ShapeDtypeStruct((CORES, Y_CHIPS, X_CHIPS, x_rows, half), jnp.float32),
        in_specs=[vmem],
        out_specs=vmem,
        scratch_shapes=[
            pltpu.VMEM((rows, half), jnp.float32),
            pltpu.VMEM((rows, half), jnp.float32),
            pltpu.VMEM((X_CHIPS, x_rows, half), jnp.float32),
            pltpu.VMEM((Z_CHIPS, x_rows // Z_CHIPS, half), jnp.float32),
            dma,
            dma,
            dma((X_CHIPS,)),
            dma((X_CHIPS,)),
            dma((Z_CHIPS,)),
            dma((Z_CHIPS,)),
            dma((Z_CHIPS,)),
            dma((Z_CHIPS,)),
            dma((2, X_CHIPS)),
            dma((2, X_CHIPS)),
            dma((2, X_CHIPS)),
            dma((2, X_CHIPS)),
            dma((13,)),
            dma((13,)),
        ],
        compiler_params=pltpu.CompilerParams(collective_id=0, has_side_effects=True),
        name="total_moments",
    )(packed)
    return out.reshape(CORES, Y_CHIPS * rows, half)


def local_kernel(place_ref, ends_ref, features_ref, tail_ref, out_ref):
    frame_rows, feat_width = features_ref.shape
    part = out_ref.shape[0] // 2
    feat = place_ref[1]
    base = place_ref[0] * frame_rows - LAG
    ends = ends_ref[...] - base
    frames = lax.broadcasted_iota(jnp.int32, (frame_rows + LAG, ends.shape[1]), 0)
    crossed = jnp.where((ends > frames) & (ends <= frames + LAG), 1.0, 0.0)
    crossed = jnp.max(crossed, axis=1, keepdims=True)
    index = lax.broadcasted_iota(jnp.int32, (frame_rows + LAG, 1), 0)
    valid = jnp.where((crossed == 0.0) & (index + base >= 0), 1.0, 0.0)
    valid = jnp.broadcast_to(valid, (frame_rows + LAG, part))
    now = valid[LAG:, :].astype(jnp.bfloat16)
    uses = (valid[LAG:, :] + valid[:frame_rows, :]).astype(jnp.bfloat16)
    lead = features_ref[:, pl.ds(pl.multiple_of(feat * part, part), part)]
    kept = lead * now
    earlier = jnp.concatenate([jnp.zeros((LAG, part), jnp.bfloat16), kept[: frame_rows - LAG, :]], axis=0)
    left = jnp.concatenate([lead * uses, earlier, uses], axis=1)
    total = contract(left, features_ref[...])
    out_ref[:part, :] = total[:part, :]
    out_ref[part:, :] = total[part : 2 * part, :] + contract(kept[frame_rows - LAG :, :], tail_ref[...])
    groups = feat_width // part
    sums = [total[2 * part : 2 * part + 1, part * m : part * m + part] for m in range(groups)]
    sums.append(jnp.zeros((8 - groups, part), jnp.float32))
    before = lax.rem(feat + groups - 1, groups) * part
    out_ref[0:8, pl.ds(pl.multiple_of(before, part), part)] = jnp.concatenate(sums, axis=0)


def local_moments(place, ends, features, tail_part, part):
    vmem = pl.BlockSpec(memory_space=pltpu.VMEM)
    return pl.pallas_call(
        local_kernel,
        out_shape=jax.ShapeDtypeStruct((2 * part, features.shape[1]), jnp.float32),
        in_specs=[pl.BlockSpec(memory_space=pltpu.SMEM), vmem, vmem, vmem],
        out_specs=vmem,
        name="local_moments",
    )(place, ends, features, tail_part)


def shards(features, seg_lengths):
    frame_rows = features.shape[0]
    feat_width = features.shape[1]
    feat_count = lax.axis_size("feat")
    tm_index = lax.axis_index("tm")
    feat_index = lax.axis_index("feat")
    col_block = feat_width // feat_count
    comp_block = NC // feat_count
    tail_part = from_behind(features[:LAG], "tm", -1)
    seg_ends = jnp.cumsum(seg_lengths).astype(jnp.int32)
    moments = tm_index * frame_rows + jnp.arange(frame_rows, dtype=jnp.int32)
    inside = (seg_ends[:, None] > moments[None, :]) & (seg_ends[:, None] <= moments[None, :] + LAG)
    validity = jnp.logical_not(jnp.any(inside, axis=0)).astype(jnp.float32)
    place = jnp.stack([tm_index, feat_index]).astype(jnp.int32)
    packed = local_moments(place, seg_ends.reshape(1, -1), features, tail_part, col_block)
    gathered = total_moments(packed)
    koopman_rows, first_part, second_part, offset = whiten(
        feat_index.astype(jnp.int32).reshape(1),
        seg_lengths.reshape(1, -1),
        gathered,
        col_block,
        comp_block,
    )
    maps = jnp.concatenate([first_part, second_part], axis=0)
    both = jnp.einsum("cf,tf->ct", maps, features, preferred_element_type=jnp.float32)
    last = jnp.einsum("cf,tf->ct", first_part, tail_part, preferred_element_type=jnp.float32)
    forward = jnp.concatenate([both[:comp_block, LAG:], last], axis=1)
    backward = both[comp_block:]
    lag_error = (forward - backward - offset[:, :1]) * validity[None, :]
    return (koopman_rows, lag_error)


def solution(mesh):
    in_specs = (P("tm", None), P())
    out_specs = (P("feat", None), P("feat", "tm"))
    return jax.shard_map(shards, mesh=mesh, in_specs=in_specs, out_specs=out_specs, check_vma=False)
```

```python
import jax
import jax.numpy as jnp
from jax import lax
from jax.experimental import pallas as pl
from jax.experimental.pallas import tpu as pltpu
from jax.sharding import PartitionSpec as P

LAG = 64
NC = 128

RIDGE = 0.05
HIGHEST = lax.Precision.HIGHEST
LEAF = 128
KERNEL_VMEM = 24 * 1024 * 1024
MESH = pl.DeviceIdType.MESH
X_CHIPS, Y_CHIPS, Z_CHIPS, CORES = 4, 4, 8, 2


def from_behind(shard, axis, by):
    count = lax.axis_size(axis)
    pairs = [(i, i + by) for i in range(count) if 0 <= i + by < count]
    return lax.ppermute(shard, axis, pairs)


def contract(left_rows, right_rows):
    return lax.dot_general(
        left_rows, right_rows, (((0,), (0,)), ((), ())), preferred_element_type=jnp.float32
    )


def exact_dot(left, right, left_dim=1, right_dim=0):
    return lax.dot_general(
        left,
        right,
        (((left_dim,), (right_dim,)), ((), ())),
        precision=HIGHEST,
        preferred_element_type=jnp.float32,
    )


def leaf_inverse(square):
    count = LEAF // 8
    tiles = [square[8 * i : 8 * i + 8, :] for i in range(count)]
    lanes = lax.broadcasted_iota(jnp.int32, (8, LEAF), 1)
    subs = lax.broadcasted_iota(jnp.int32, (8, LEAF), 0)

    def spread(tile, sub):
        return jnp.broadcast_to(tile[sub : sub + 1, :], (8, LEAF))

    for g in range(count):
        first = 8 * g
        own = tiles[g]
        columns = [jnp.broadcast_to(own[:, first + k : first + k + 1], (8, LEAF)) for k in range(8)]
        in_block = (lanes >= first) & (lanes < first + 8)
        rows = jnp.where(in_block, jnp.where(lanes - first == subs, 1.0, 0.0), own)
        pivots = columns[0]
        if g + 1 < count:
            after = tiles[g + 1]
            after_columns = [
                jnp.broadcast_to(after[:, first + k : first + k + 1], (8, LEAF)) for k in range(8)
            ]
            after = jnp.where(in_block, 0.0, after)
        for k in range(8):
            corner_rows = [spread(columns[m], k) for m in range(k, 8)]
            row = spread(rows, k)
            flip = 1.0 / corner_rows[0]
            pivots = jnp.where(subs == k, columns[k], pivots)
            factor = jnp.where(subs > k, columns[k] * flip, 0.0)
            rows = rows - factor * row
            for m in range(k + 1, 8):
                columns[m] = columns[m] - factor * corner_rows[m - k]
            if g + 1 < count:
                factor = after_columns[k] * flip
                after = after - factor * row
                for m in range(k + 1, 8):
                    after_columns[m] = after_columns[m] - factor * corner_rows[m - k]
        rows = rows * lax.rsqrt(pivots)
        tiles[g] = rows
        if g + 1 < count:
            tiles[g + 1] = after
        if g + 2 < count:
            turned = rows.T
            spreads = [spread(rows, k) for k in range(8)]
            for i in range(g + 2, count):
                tile = jnp.where(in_block, 0.0, tiles[i])
                for k in range(8):
                    tile = tile - jnp.broadcast_to(turned[8 * i : 8 * i + 8, k : k + 1], (8, LEAF)) * spreads[k]
                tiles[i] = tile
    outs = [jnp.where(lanes <= subs + 8 * i, tiles[i], 0.0) for i in range(count)]
    return jnp.concatenate(outs, axis=0)


def whiten_kernel(
    index_ref, lengths_ref, moments_ref, koop_ref, first_ref, second_ref, offset_ref, work, cov
):
    feat_width = work.shape[0]
    blocks = feat_width // LEAF
    part = koop_ref.shape[0]
    pairs = jnp.maximum(lengths_ref[...] - LAG, 0).astype(jnp.float32)
    scale = 1.0 / (2.0 * jnp.sum(pairs, axis=1, keepdims=True))

    def moment(kind, k, m):
        top, left = LEAF * (2 * k + kind), LEAF * (m % 2)
        return moments_ref[m // 2, top : top + LEAF, left : left + LEAF]

    def gram_block(k, m):
        return moment(0, m, k).T if m == (k + blocks - 1) % blocks else moment(0, k, m)

    sums = moment(0, 0, blocks - 1)
    mean = jnp.concatenate([sums[m : m + 1, :] for m in range(blocks)], axis=1) * scale
    mean_cols = jnp.broadcast_to(mean, (LEAF, feat_width)).T
    rows_io = lax.broadcasted_iota(jnp.int32, (LEAF, LEAF), 0)
    lanes_io = lax.broadcasted_iota(jnp.int32, (LEAF, LEAF), 1)
    eye = rows_io == lanes_io
    trace = jnp.zeros((1, 1), jnp.float32)
    for k in range(blocks):
        square = gram_block(k, k) * scale - mean_cols[LEAF * k : LEAF * k + LEAF, :] * mean[:, LEAF * k : LEAF * k + LEAF]
        diag = jnp.sum(jnp.where(eye, square, 0.0), axis=0, keepdims=True)
        trace = trace + jnp.sum(diag, axis=1, keepdims=True)
    ridge = RIDGE * (trace / feat_width)
    for k in range(blocks):
        for m in range(blocks):
            outer = mean_cols[LEAF * k : LEAF * k + LEAF, :] * mean[:, LEAF * m : LEAF * m + LEAF]
            block = gram_block(k, m) * scale - outer
            if k == m:
                block = block + jnp.where(eye, ridge, 0.0)
            work[LEAF * k : LEAF * k + LEAF, LEAF * m : LEAF * m + LEAF] = block
            straight = moment(1, k, m)
            turned = moment(1, m, k).T
            cov[LEAF * k : LEAF * k + LEAF, LEAF * m : LEAF * m + LEAF] = (straight + turned) * scale - outer

    def eliminate(k, carry):
        start = pl.multiple_of(k * LEAF, LEAF)
        inverse = leaf_inverse(work[pl.ds(start, LEAF), pl.ds(start, LEAF)])
        work[pl.ds(start, LEAF), pl.ds(start, LEAF)] = jnp.where(eye, 1.0, 0.0)
        panel = exact_dot(inverse, work[pl.ds(start, LEAF), :])
        wide_lanes = lax.broadcasted_iota(jnp.int32, (LEAF, feat_width), 1)
        in_block = (wide_lanes >= start) & (wide_lanes < start + LEAF)
        for i in range(1, blocks):

            @pl.when(k < i)
            def _(i=i):
                old = jnp.where(in_block, 0.0, work[LEAF * i : LEAF * i + LEAF, :])
                change = exact_dot(panel[:, LEAF * i : LEAF * i + LEAF], panel, 0, 0)
                work[LEAF * i : LEAF * i + LEAF, :] = old - change

        work[pl.ds(start, LEAF), :] = panel
        return carry

    lax.fori_loop(0, blocks, eliminate, 0)
    rows_io = lax.broadcasted_iota(jnp.int32, (feat_width, feat_width), 0)
    lanes_io = lax.broadcasted_iota(jnp.int32, (feat_width, feat_width), 1)
    work[...] = jnp.where(rows_io >= lanes_io, work[...], 0.0)
    index = index_ref[0]
    comps = first_ref.shape[0]
    own_rows = work[pl.ds(pl.multiple_of(index * part, part), part), :]
    own_comps = work[pl.ds(pl.multiple_of(index * comps, comps), comps), :]
    stacked = jnp.concatenate([own_rows, own_comps], axis=0)
    koop = exact_dot(exact_dot(stacked, cov[...]), work[...], 1, 1)
    koop_ref[...] = koop[:part, :]
    first = own_comps.astype(jnp.bfloat16)
    second = exact_dot(koop[part:, :], work[...]).astype(jnp.bfloat16)
    first_ref[...] = first
    second_ref[...] = second
    gap = (first.astype(jnp.float32) - second.astype(jnp.float32)) * mean
    offset_ref[...] = jnp.broadcast_to(jnp.sum(gap, axis=1, keepdims=True), offset_ref.shape)


def whiten(index, lengths, moments, part, comps):
    feat_width = 2 * moments.shape[2]
    vmem = pl.BlockSpec(memory_space=pltpu.VMEM)
    return pl.pallas_call(
        whiten_kernel,
        out_shape=(
            jax.ShapeDtypeStruct((part, feat_width), jnp.float32),
            jax.ShapeDtypeStruct((comps, feat_width), jnp.bfloat16),
            jax.ShapeDtypeStruct((comps, feat_width), jnp.bfloat16),
            jax.ShapeDtypeStruct((comps, 128), jnp.float32),
        ),
        in_specs=[pl.BlockSpec(memory_space=pltpu.SMEM), vmem, vmem],
        out_specs=(vmem, vmem, vmem, vmem),
        scratch_shapes=[
            pltpu.VMEM((feat_width, feat_width), jnp.float32),
            pltpu.VMEM((feat_width, feat_width), jnp.float32),
        ],
        compiler_params=pltpu.CompilerParams(vmem_limit_bytes=KERNEL_VMEM),
        name="whiten",
    )(index, lengths, moments)


def total_kernel(
    mine_ref, out_ref, from_core, held, from_x, from_z, core_send, core_recv, x_send, x_recv, z_send, z_recv,
    gz_send, gz_recv, ga_send, ga_recv, gb_send, gb_recv, gc_send, gc_recv
):
    place, y = lax.axis_index("tm"), lax.axis_index("feat")
    core = lax.rem(place, CORES)
    z = lax.rem(lax.div(place, CORES), Z_CHIPS)
    x = lax.div(place, CORES * Z_CHIPS)
    rows, half = held.shape
    x_rows = rows // X_CHIPS
    z_rows = x_rows // Z_CHIPS
    split = x_rows // 2

    def at(x_to, z_to, core_to):
        return {"tm": (x_to * Z_CHIPS + z_to) * CORES + core_to}

    def along_x(step):
        return at(lax.rem(x + step, X_CHIPS), z, core)

    def along_z(step):
        return at(x, lax.rem(z + step, Z_CHIPS), core)

    def along_y(step):
        return {"feat": lax.rem(y + step, Y_CHIPS)}

    partner = at(x, z, 1 - core)
    peers = [partner]
    peers += [along_x(step) for step in range(1, X_CHIPS)]
    peers += [along_z(step) for step in range(1, Z_CHIPS)]
    peers += [along_y(step) for step in range(1, Y_CHIPS)]
    barrier = pltpu.get_barrier_semaphore()
    for peer in peers:
        pl.semaphore_signal(barrier, inc=1, device_id=peer, device_id_type=MESH)
    pl.semaphore_wait(barrier, len(peers))

    def send(src, dst, send_sem, recv_sem, peer):
        copy = pltpu.make_async_remote_copy(
            src_ref=src, dst_ref=dst, send_sem=send_sem, recv_sem=recv_sem, device_id=peer, device_id_type=MESH
        )
        copy.start()
        return copy

    def finish(copies):
        for copy in copies:
            copy.wait()

    other_lanes = pl.ds(pl.multiple_of((1 - core) * half, half), half)
    own_lanes = pl.ds(pl.multiple_of(core * half, half), half)
    finish([send(mine_ref.at[:, other_lanes], from_core, core_send, core_recv, partner)])
    held[...] = mine_ref[:, own_lanes] + from_core[...]

    copies = []
    for step in range(1, X_CHIPS):
        to = pl.multiple_of(lax.rem(x + step, X_CHIPS) * x_rows, x_rows)
        copies.append(
            send(held.at[pl.ds(to, x_rows), :], from_x.at[step], x_send.at[step], x_recv.at[step], along_x(step))
        )
    finish(copies)
    total = held[pl.ds(pl.multiple_of(x * x_rows, x_rows), x_rows), :]
    for step in range(1, X_CHIPS):
        total = total + from_x[step]
    from_x[0] = total

    copies = []
    for step in range(1, Z_CHIPS):
        to = pl.multiple_of(lax.rem(z + step, Z_CHIPS) * z_rows, z_rows)
        copies.append(
            send(from_x.at[0, pl.ds(to, z_rows), :], from_z.at[step], z_send.at[step], z_recv.at[step], along_z(step))
        )
    finish(copies)
    own = pl.ds(pl.multiple_of(z * z_rows, z_rows), z_rows)
    total = from_x[0, own, :]
    for step in range(1, Z_CHIPS):
        total = total + from_z[step]
    out_ref[core, y, x, own, :] = total

    piece = out_ref.at[core, y, x, own, :]
    finish(
        [send(piece, piece, gz_send.at[step], gz_recv.at[step], along_z(step)) for step in range(1, Z_CHIPS)]
    )
    low, high = pl.ds(0, split), pl.ds(split, split)
    forwarded = []

    def forward(piece):
        slot = len(forwarded)
        forwarded.append(send(piece, piece, gc_send.at[slot], gc_recv.at[slot], partner))

    def back(place, step, count):
        return lax.rem(place + count - step, count)

    first_x, first_y, next_x, next_y = [], [], [], []
    piece = out_ref.at[core, y, x, low, :]
    for step in range(1, X_CHIPS):
        first_x.append(send(piece, piece, ga_send.at[0, step], ga_recv.at[0, step], along_x(step)))
    piece = out_ref.at[core, y, x, high, :]
    for step in range(1, Y_CHIPS):
        first_y.append(send(piece, piece, ga_send.at[1, step], ga_recv.at[1, step], along_y(step)))
    forward(out_ref.at[core, y, x])
    finish(first_x)
    piece = out_ref.at[core, y, :, low, :]
    for step in range(1, Y_CHIPS):
        next_y.append(send(piece, piece, gb_send.at[0, step], gb_recv.at[0, step], along_y(step)))
    finish(first_y)
    piece = out_ref.at[core, :, x, high, :]
    for step in range(1, X_CHIPS):
        next_x.append(send(piece, piece, gb_send.at[1, step], gb_recv.at[1, step], along_x(step)))
    for step in range(1, X_CHIPS):
        forward(out_ref.at[core, y, back(x, step, X_CHIPS), low, :])
    for step in range(1, Y_CHIPS):
        forward(out_ref.at[core, back(y, step, Y_CHIPS), x, high, :])
    for step in (1, 3, 2):
        next_y[step - 1].wait()
        forward(out_ref.at[core, back(y, step, Y_CHIPS), :, low, :])
        next_x[step - 1].wait()
        forward(out_ref.at[core, :, back(x, step, X_CHIPS), high, :])
    finish(forwarded)


def total_moments(packed):
    rows, width = packed.shape
    half, x_rows = width // CORES, rows // X_CHIPS
    vmem = pl.BlockSpec(memory_space=pltpu.VMEM)
    dma = pltpu.SemaphoreType.DMA
    out = pl.pallas_call(
        total_kernel,
        out_shape=jax.ShapeDtypeStruct((CORES, Y_CHIPS, X_CHIPS, x_rows, half), jnp.float32),
        in_specs=[vmem],
        out_specs=vmem,
        scratch_shapes=[
            pltpu.VMEM((rows, half), jnp.float32),
            pltpu.VMEM((rows, half), jnp.float32),
            pltpu.VMEM((X_CHIPS, x_rows, half), jnp.float32),
            pltpu.VMEM((Z_CHIPS, x_rows // Z_CHIPS, half), jnp.float32),
            dma,
            dma,
            dma((X_CHIPS,)),
            dma((X_CHIPS,)),
            dma((Z_CHIPS,)),
            dma((Z_CHIPS,)),
            dma((Z_CHIPS,)),
            dma((Z_CHIPS,)),
            dma((2, X_CHIPS)),
            dma((2, X_CHIPS)),
            dma((2, X_CHIPS)),
            dma((2, X_CHIPS)),
            dma((13,)),
            dma((13,)),
        ],
        compiler_params=pltpu.CompilerParams(
            collective_id=0, has_side_effects=True, vmem_limit_bytes=KERNEL_VMEM
        ),
        name="total_moments",
    )(packed)
    return out.reshape(CORES, Y_CHIPS * rows, half)


def local_kernel(place_ref, ends_ref, features_ref, tail_ref, out_ref):
    frame_rows, feat_width = features_ref.shape
    part = out_ref.shape[0] // 2
    feat = place_ref[1]
    base = place_ref[0] * frame_rows - LAG
    ends = ends_ref[...] - base
    frames = lax.broadcasted_iota(jnp.int32, (frame_rows + LAG, ends.shape[1]), 0)
    crossed = jnp.where((ends > frames) & (ends <= frames + LAG), 1.0, 0.0)
    crossed = jnp.max(crossed, axis=1, keepdims=True)
    index = lax.broadcasted_iota(jnp.int32, (frame_rows + LAG, 1), 0)
    valid = jnp.where((crossed == 0.0) & (index + base >= 0), 1.0, 0.0)
    valid = jnp.broadcast_to(valid, (frame_rows + LAG, part))
    now = valid[LAG:, :].astype(jnp.bfloat16)
    uses = (valid[LAG:, :] + valid[:frame_rows, :]).astype(jnp.bfloat16)
    lead = features_ref[:, pl.ds(pl.multiple_of(feat * part, part), part)]
    kept = lead * now
    earlier = jnp.concatenate([jnp.zeros((LAG, part), jnp.bfloat16), kept[: frame_rows - LAG, :]], axis=0)
    left = jnp.concatenate([lead * uses, earlier, uses], axis=1)
    total = contract(left, features_ref[...])
    out_ref[:part, :] = total[:part, :]
    out_ref[part:, :] = total[part : 2 * part, :] + contract(kept[frame_rows - LAG :, :], tail_ref[...])
    groups = feat_width // part
    sums = [total[2 * part : 2 * part + 1, part * m : part * m + part] for m in range(groups)]
    sums.append(jnp.zeros((8 - groups, part), jnp.float32))
    before = lax.rem(feat + groups - 1, groups) * part
    out_ref[0:8, pl.ds(pl.multiple_of(before, part), part)] = jnp.concatenate(sums, axis=0)


def local_moments(place, ends, features, tail_part, part):
    vmem = pl.BlockSpec(memory_space=pltpu.VMEM)
    return pl.pallas_call(
        local_kernel,
        out_shape=jax.ShapeDtypeStruct((2 * part, features.shape[1]), jnp.float32),
        in_specs=[pl.BlockSpec(memory_space=pltpu.SMEM), vmem, vmem, vmem],
        out_specs=vmem,
        compiler_params=pltpu.CompilerParams(vmem_limit_bytes=KERNEL_VMEM),
        name="local_moments",
    )(place, ends, features, tail_part)


def shards(features, seg_lengths):
    frame_rows = features.shape[0]
    feat_width = features.shape[1]
    feat_count = lax.axis_size("feat")
    tm_index = lax.axis_index("tm")
    feat_index = lax.axis_index("feat")
    col_block = feat_width // feat_count
    comp_block = NC // feat_count
    tail_part = from_behind(features[:LAG], "tm", -1)
    seg_ends = jnp.cumsum(seg_lengths).astype(jnp.int32)
    moments = tm_index * frame_rows + jnp.arange(frame_rows, dtype=jnp.int32)
    inside = (seg_ends[:, None] > moments[None, :]) & (seg_ends[:, None] <= moments[None, :] + LAG)
    validity = jnp.logical_not(jnp.any(inside, axis=0)).astype(jnp.float32)
    place = jnp.stack([tm_index, feat_index]).astype(jnp.int32)
    packed = local_moments(place, seg_ends.reshape(1, -1), features, tail_part, col_block)
    gathered = total_moments(packed)
    koopman_rows, first_part, second_part, offset = whiten(
        feat_index.astype(jnp.int32).reshape(1),
        seg_lengths.reshape(1, -1),
        gathered,
        col_block,
        comp_block,
    )
    maps = jnp.concatenate([first_part, second_part], axis=0)
    both = jnp.einsum("cf,tf->ct", maps, features, preferred_element_type=jnp.float32)
    last = jnp.einsum("cf,tf->ct", first_part, tail_part, preferred_element_type=jnp.float32)
    forward = jnp.concatenate([both[:comp_block, LAG:], last], axis=1)
    backward = both[comp_block:]
    lag_error = (forward - backward - offset[:, :1]) * validity[None, :]
    return (koopman_rows, lag_error)


def solution(mesh):
    in_specs = (P("tm", None), P())
    out_specs = (P("feat", None), P("feat", "tm"))
    return jax.shard_map(shards, mesh=mesh, in_specs=in_specs, out_specs=out_specs, check_vma=False)
```

```python
import jax
import jax.numpy as jnp
from jax import lax
from jax.experimental import pallas as pl
from jax.experimental.pallas import tpu as pltpu
from jax.sharding import PartitionSpec as P

LAG = 64
NC = 128

RIDGE = 0.05
HIGHEST = lax.Precision.HIGHEST
LEAF = 128
KERNEL_VMEM = 24 * 1024 * 1024
MESH = pl.DeviceIdType.MESH
X_CHIPS, Y_CHIPS, Z_CHIPS, CORES = 4, 4, 8, 2


def from_behind(shard, axis, by):
    count = lax.axis_size(axis)
    pairs = [(i, i + by) for i in range(count) if 0 <= i + by < count]
    return lax.ppermute(shard, axis, pairs)


def contract(left_rows, right_rows):
    return lax.dot_general(
        left_rows, right_rows, (((0,), (0,)), ((), ())), preferred_element_type=jnp.float32
    )


def exact_dot(left, right, left_dim=1, right_dim=0):
    return lax.dot_general(
        left,
        right,
        (((left_dim,), (right_dim,)), ((), ())),
        precision=HIGHEST,
        preferred_element_type=jnp.float32,
    )


def leaf_inverse(square):
    count = LEAF // 8
    tiles = [square[8 * i : 8 * i + 8, :] for i in range(count)]
    lanes = lax.broadcasted_iota(jnp.int32, (8, LEAF), 1)
    subs = lax.broadcasted_iota(jnp.int32, (8, LEAF), 0)

    def spread(tile, sub):
        return jnp.broadcast_to(tile[sub : sub + 1, :], (8, LEAF))

    for g in range(count):
        first = 8 * g
        own = tiles[g]
        columns = [jnp.broadcast_to(own[:, first + k : first + k + 1], (8, LEAF)) for k in range(8)]
        in_block = (lanes >= first) & (lanes < first + 8)
        rows = jnp.where(in_block, jnp.where(lanes - first == subs, 1.0, 0.0), own)
        pivots = columns[0]
        if g + 1 < count:
            after = tiles[g + 1]
            after_columns = [
                jnp.broadcast_to(after[:, first + k : first + k + 1], (8, LEAF)) for k in range(8)
            ]
            after = jnp.where(in_block, 0.0, after)
        for k in range(8):
            corner_rows = [spread(columns[m], k) for m in range(k, 8)]
            row = spread(rows, k)
            flip = 1.0 / corner_rows[0]
            pivots = jnp.where(subs == k, columns[k], pivots)
            factor = jnp.where(subs > k, columns[k] * flip, 0.0)
            rows = rows - factor * row
            for m in range(k + 1, 8):
                columns[m] = columns[m] - factor * corner_rows[m - k]
            if g + 1 < count:
                factor = after_columns[k] * flip
                after = after - factor * row
                for m in range(k + 1, 8):
                    after_columns[m] = after_columns[m] - factor * corner_rows[m - k]
        rows = rows * lax.rsqrt(pivots)
        tiles[g] = rows
        if g + 1 < count:
            tiles[g + 1] = after
        if g + 2 < count:
            turned = rows.T
            spreads = [spread(rows, k) for k in range(8)]
            for i in range(g + 2, count):
                tile = jnp.where(in_block, 0.0, tiles[i])
                for k in range(8):
                    tile = tile - jnp.broadcast_to(turned[8 * i : 8 * i + 8, k : k + 1], (8, LEAF)) * spreads[k]
                tiles[i] = tile
    outs = [jnp.where(lanes <= subs + 8 * i, tiles[i], 0.0) for i in range(count)]
    return jnp.concatenate(outs, axis=0)


def whiten_kernel(
    index_ref, lengths_ref, moments_ref, koop_ref, first_ref, second_ref, offset_ref, work, cov
):
    feat_width = work.shape[0]
    blocks = feat_width // LEAF
    part = koop_ref.shape[0]
    pairs = jnp.maximum(lengths_ref[...] - LAG, 0).astype(jnp.float32)
    scale = 1.0 / (2.0 * jnp.sum(pairs, axis=1, keepdims=True))

    def moment(kind, k, m):
        top, left = LEAF * (2 * k + kind), LEAF * (m % 2)
        return moments_ref[m // 2, top : top + LEAF, left : left + LEAF]

    def gram_block(k, m):
        return moment(0, m, k).T if m == (k + blocks - 1) % blocks else moment(0, k, m)

    sums = moment(0, 0, blocks - 1)
    mean = jnp.concatenate([sums[m : m + 1, :] for m in range(blocks)], axis=1) * scale
    mean_cols = jnp.broadcast_to(mean, (LEAF, feat_width)).T
    rows_io = lax.broadcasted_iota(jnp.int32, (LEAF, LEAF), 0)
    lanes_io = lax.broadcasted_iota(jnp.int32, (LEAF, LEAF), 1)
    eye = rows_io == lanes_io
    trace = jnp.zeros((1, 1), jnp.float32)
    for k in range(blocks):
        square = gram_block(k, k) * scale - mean_cols[LEAF * k : LEAF * k + LEAF, :] * mean[:, LEAF * k : LEAF * k + LEAF]
        diag = jnp.sum(jnp.where(eye, square, 0.0), axis=0, keepdims=True)
        trace = trace + jnp.sum(diag, axis=1, keepdims=True)
    ridge = RIDGE * (trace / feat_width)
    for k in range(blocks):
        for m in range(blocks):
            outer = mean_cols[LEAF * k : LEAF * k + LEAF, :] * mean[:, LEAF * m : LEAF * m + LEAF]
            block = gram_block(k, m) * scale - outer
            if k == m:
                block = block + jnp.where(eye, ridge, 0.0)
            work[LEAF * k : LEAF * k + LEAF, LEAF * m : LEAF * m + LEAF] = block
            straight = moment(1, k, m)
            turned = moment(1, m, k).T
            cov[LEAF * k : LEAF * k + LEAF, LEAF * m : LEAF * m + LEAF] = (straight + turned) * scale - outer

    def eliminate(k, carry):
        start = pl.multiple_of(k * LEAF, LEAF)
        inverse = leaf_inverse(work[pl.ds(start, LEAF), pl.ds(start, LEAF)])
        work[pl.ds(start, LEAF), pl.ds(start, LEAF)] = jnp.where(eye, 1.0, 0.0)
        panel = exact_dot(inverse, work[pl.ds(start, LEAF), :])
        wide_lanes = lax.broadcasted_iota(jnp.int32, (LEAF, feat_width), 1)
        in_block = (wide_lanes >= start) & (wide_lanes < start + LEAF)
        for i in range(1, blocks):

            @pl.when(k < i)
            def _(i=i):
                old = jnp.where(in_block, 0.0, work[LEAF * i : LEAF * i + LEAF, :])
                change = exact_dot(panel[:, LEAF * i : LEAF * i + LEAF], panel, 0, 0)
                work[LEAF * i : LEAF * i + LEAF, :] = old - change

        work[pl.ds(start, LEAF), :] = panel
        return carry

    lax.fori_loop(0, blocks, eliminate, 0)
    rows_io = lax.broadcasted_iota(jnp.int32, (feat_width, feat_width), 0)
    lanes_io = lax.broadcasted_iota(jnp.int32, (feat_width, feat_width), 1)
    work[...] = jnp.where(rows_io >= lanes_io, work[...], 0.0)
    index = index_ref[0]
    comps = first_ref.shape[0]
    own_rows = work[pl.ds(pl.multiple_of(index * part, part), part), :]
    own_comps = work[pl.ds(pl.multiple_of(index * comps, comps), comps), :]
    stacked = jnp.concatenate([own_rows, own_comps], axis=0)
    koop = exact_dot(exact_dot(stacked, cov[...]), work[...], 1, 1)
    koop_ref[...] = koop[:part, :]
    first = own_comps.astype(jnp.bfloat16)
    second = exact_dot(koop[part:, :], work[...]).astype(jnp.bfloat16)
    first_ref[...] = first
    second_ref[...] = second
    gap = (first.astype(jnp.float32) - second.astype(jnp.float32)) * mean
    offset_ref[...] = jnp.broadcast_to(jnp.sum(gap, axis=1, keepdims=True), offset_ref.shape)


def whiten(index, lengths, moments, part, comps):
    feat_width = 2 * moments.shape[2]
    vmem = pl.BlockSpec(memory_space=pltpu.VMEM)
    return pl.pallas_call(
        whiten_kernel,
        out_shape=(
            jax.ShapeDtypeStruct((part, feat_width), jnp.float32),
            jax.ShapeDtypeStruct((comps, feat_width), jnp.bfloat16),
            jax.ShapeDtypeStruct((comps, feat_width), jnp.bfloat16),
            jax.ShapeDtypeStruct((comps, 128), jnp.float32),
        ),
        in_specs=[pl.BlockSpec(memory_space=pltpu.SMEM), vmem, vmem],
        out_specs=(vmem, vmem, vmem, vmem),
        scratch_shapes=[
            pltpu.VMEM((feat_width, feat_width), jnp.float32),
            pltpu.VMEM((feat_width, feat_width), jnp.float32),
        ],
        compiler_params=pltpu.CompilerParams(vmem_limit_bytes=KERNEL_VMEM),
        name="whiten",
    )(index, lengths, moments)


def total_kernel(
    mine_ref, out_ref, from_core, held, from_x, from_z, core_send, core_recv, x_send, x_recv, z_send, z_recv,
    gz_send, gz_recv, ga_send, ga_recv, gb_send, gb_recv, gc_send, gc_recv
):
    place, y = lax.axis_index("tm"), lax.axis_index("feat")
    core = lax.rem(place, CORES)
    z = lax.rem(lax.div(place, CORES), Z_CHIPS)
    x = lax.div(place, CORES * Z_CHIPS)
    rows, half = held.shape
    x_rows = rows // X_CHIPS
    z_rows = x_rows // Z_CHIPS
    split = x_rows // 2

    def at(x_to, z_to, core_to):
        return {"tm": (x_to * Z_CHIPS + z_to) * CORES + core_to}

    def along_x(step):
        return at(lax.rem(x + step, X_CHIPS), z, core)

    def along_z(step):
        return at(x, lax.rem(z + step, Z_CHIPS), core)

    def along_y(step):
        return {"feat": lax.rem(y + step, Y_CHIPS)}

    partner = at(x, z, 1 - core)
    peers = [partner]
    peers += [along_x(step) for step in range(1, X_CHIPS)]
    peers += [along_z(step) for step in range(1, Z_CHIPS)]
    peers += [along_y(step) for step in range(1, Y_CHIPS)]
    barrier = pltpu.get_barrier_semaphore()
    for peer in peers:
        pl.semaphore_signal(barrier, inc=1, device_id=peer, device_id_type=MESH)
    pl.semaphore_wait(barrier, len(peers))

    def send(src, dst, send_sem, recv_sem, peer):
        copy = pltpu.make_async_remote_copy(
            src_ref=src, dst_ref=dst, send_sem=send_sem, recv_sem=recv_sem, device_id=peer, device_id_type=MESH
        )
        copy.start()
        return copy

    def finish(copies):
        for copy in copies:
            copy.wait()

    other_lanes = pl.ds(pl.multiple_of((1 - core) * half, half), half)
    own_lanes = pl.ds(pl.multiple_of(core * half, half), half)
    order = [2, 1, 3, 0]
    chunks = [pl.ds(pl.multiple_of(lax.rem(x + step, X_CHIPS) * x_rows, x_rows), x_rows) for step in range(X_CHIPS)]
    swaps = {}
    for step in order:
        swaps[step] = send(
            mine_ref.at[chunks[step], other_lanes], from_core.at[chunks[step], :],
            core_send.at[step], core_recv.at[step], partner
        )
    copies = []
    for step in order:
        swaps[step].wait()
        held[chunks[step], :] = mine_ref[chunks[step], own_lanes] + from_core[chunks[step], :]
        if step:
            copies.append(
                send(held.at[chunks[step], :], from_x.at[step], x_send.at[step], x_recv.at[step], along_x(step))
            )
    finish(copies)
    total = held[pl.ds(pl.multiple_of(x * x_rows, x_rows), x_rows), :]
    for step in range(1, X_CHIPS):
        total = total + from_x[step]
    from_x[0] = total

    copies = []
    for step in range(1, Z_CHIPS):
        to = pl.multiple_of(lax.rem(z + step, Z_CHIPS) * z_rows, z_rows)
        copies.append(
            send(from_x.at[0, pl.ds(to, z_rows), :], from_z.at[step], z_send.at[step], z_recv.at[step], along_z(step))
        )
    finish(copies)
    own = pl.ds(pl.multiple_of(z * z_rows, z_rows), z_rows)
    total = from_x[0, own, :]
    for step in range(1, Z_CHIPS):
        total = total + from_z[step]
    out_ref[core, y, x, own, :] = total

    piece = out_ref.at[core, y, x, own, :]
    finish(
        [send(piece, piece, gz_send.at[step], gz_recv.at[step], along_z(step)) for step in range(1, Z_CHIPS)]
    )
    low, high = pl.ds(0, split), pl.ds(split, split)
    forwarded = []

    def forward(piece):
        slot = len(forwarded)
        forwarded.append(send(piece, piece, gc_send.at[slot], gc_recv.at[slot], partner))

    def back(place, step, count):
        return lax.rem(place + count - step, count)

    first_x, first_y, next_x, next_y = [], [], [], []
    piece = out_ref.at[core, y, x, low, :]
    for step in range(1, X_CHIPS):
        first_x.append(send(piece, piece, ga_send.at[0, step], ga_recv.at[0, step], along_x(step)))
    piece = out_ref.at[core, y, x, high, :]
    for step in range(1, Y_CHIPS):
        first_y.append(send(piece, piece, ga_send.at[1, step], ga_recv.at[1, step], along_y(step)))
    forward(out_ref.at[core, y, x])
    finish(first_x)
    piece = out_ref.at[core, y, :, low, :]
    for step in range(1, Y_CHIPS):
        next_y.append(send(piece, piece, gb_send.at[0, step], gb_recv.at[0, step], along_y(step)))
    finish(first_y)
    piece = out_ref.at[core, :, x, high, :]
    for step in range(1, X_CHIPS):
        next_x.append(send(piece, piece, gb_send.at[1, step], gb_recv.at[1, step], along_x(step)))
    for step in range(1, X_CHIPS):
        forward(out_ref.at[core, y, back(x, step, X_CHIPS), low, :])
    for step in range(1, Y_CHIPS):
        forward(out_ref.at[core, back(y, step, Y_CHIPS), x, high, :])
    for step in (1, 3, 2):
        next_y[step - 1].wait()
        forward(out_ref.at[core, back(y, step, Y_CHIPS), :, low, :])
        next_x[step - 1].wait()
        forward(out_ref.at[core, :, back(x, step, X_CHIPS), high, :])
    finish(forwarded)


def total_moments(packed):
    rows, width = packed.shape
    half, x_rows = width // CORES, rows // X_CHIPS
    vmem = pl.BlockSpec(memory_space=pltpu.VMEM)
    dma = pltpu.SemaphoreType.DMA
    out = pl.pallas_call(
        total_kernel,
        out_shape=jax.ShapeDtypeStruct((CORES, Y_CHIPS, X_CHIPS, x_rows, half), jnp.float32),
        in_specs=[vmem],
        out_specs=vmem,
        scratch_shapes=[
            pltpu.VMEM((rows, half), jnp.float32),
            pltpu.VMEM((rows, half), jnp.float32),
            pltpu.VMEM((X_CHIPS, x_rows, half), jnp.float32),
            pltpu.VMEM((Z_CHIPS, x_rows // Z_CHIPS, half), jnp.float32),
            dma((X_CHIPS,)),
            dma((X_CHIPS,)),
            dma((X_CHIPS,)),
            dma((X_CHIPS,)),
            dma((Z_CHIPS,)),
            dma((Z_CHIPS,)),
            dma((Z_CHIPS,)),
            dma((Z_CHIPS,)),
            dma((2, X_CHIPS)),
            dma((2, X_CHIPS)),
            dma((2, X_CHIPS)),
            dma((2, X_CHIPS)),
            dma((13,)),
            dma((13,)),
        ],
        compiler_params=pltpu.CompilerParams(
            collective_id=0, has_side_effects=True, vmem_limit_bytes=KERNEL_VMEM
        ),
        name="total_moments",
    )(packed)
    return out.reshape(CORES, Y_CHIPS * rows, half)


def local_kernel(place_ref, ends_ref, features_ref, tail_ref, out_ref):
    frame_rows, feat_width = features_ref.shape
    part = out_ref.shape[0] // 2
    feat = place_ref[1]
    base = place_ref[0] * frame_rows - LAG
    ends = ends_ref[...] - base
    frames = lax.broadcasted_iota(jnp.int32, (frame_rows + LAG, ends.shape[1]), 0)
    crossed = jnp.where((ends > frames) & (ends <= frames + LAG), 1.0, 0.0)
    crossed = jnp.max(crossed, axis=1, keepdims=True)
    index = lax.broadcasted_iota(jnp.int32, (frame_rows + LAG, 1), 0)
    valid = jnp.where((crossed == 0.0) & (index + base >= 0), 1.0, 0.0)
    valid = jnp.broadcast_to(valid, (frame_rows + LAG, part))
    now = valid[LAG:, :].astype(jnp.bfloat16)
    uses = (valid[LAG:, :] + valid[:frame_rows, :]).astype(jnp.bfloat16)
    lead = features_ref[:, pl.ds(pl.multiple_of(feat * part, part), part)]
    kept = lead * now
    earlier = jnp.concatenate([jnp.zeros((LAG, part), jnp.bfloat16), kept[: frame_rows - LAG, :]], axis=0)
    left = jnp.concatenate([lead * uses, earlier, uses], axis=1)
    total = contract(left, features_ref[...])
    out_ref[:part, :] = total[:part, :]
    out_ref[part:, :] = total[part : 2 * part, :] + contract(kept[frame_rows - LAG :, :], tail_ref[...])
    groups = feat_width // part
    sums = [total[2 * part : 2 * part + 1, part * m : part * m + part] for m in range(groups)]
    sums.append(jnp.zeros((8 - groups, part), jnp.float32))
    before = lax.rem(feat + groups - 1, groups) * part
    out_ref[0:8, pl.ds(pl.multiple_of(before, part), part)] = jnp.concatenate(sums, axis=0)


def local_moments(place, ends, features, tail_part, part):
    vmem = pl.BlockSpec(memory_space=pltpu.VMEM)
    return pl.pallas_call(
        local_kernel,
        out_shape=jax.ShapeDtypeStruct((2 * part, features.shape[1]), jnp.float32),
        in_specs=[pl.BlockSpec(memory_space=pltpu.SMEM), vmem, vmem, vmem],
        out_specs=vmem,
        compiler_params=pltpu.CompilerParams(vmem_limit_bytes=KERNEL_VMEM),
        name="local_moments",
    )(place, ends, features, tail_part)


def shards(features, seg_lengths):
    frame_rows = features.shape[0]
    feat_width = features.shape[1]
    feat_count = lax.axis_size("feat")
    tm_index = lax.axis_index("tm")
    feat_index = lax.axis_index("feat")
    col_block = feat_width // feat_count
    comp_block = NC // feat_count
    tail_part = from_behind(features[:LAG], "tm", -1)
    seg_ends = jnp.cumsum(seg_lengths).astype(jnp.int32)
    moments = tm_index * frame_rows + jnp.arange(frame_rows, dtype=jnp.int32)
    inside = (seg_ends[:, None] > moments[None, :]) & (seg_ends[:, None] <= moments[None, :] + LAG)
    validity = jnp.logical_not(jnp.any(inside, axis=0)).astype(jnp.float32)
    place = jnp.stack([tm_index, feat_index]).astype(jnp.int32)
    packed = local_moments(place, seg_ends.reshape(1, -1), features, tail_part, col_block)
    gathered = total_moments(packed)
    koopman_rows, first_part, second_part, offset = whiten(
        feat_index.astype(jnp.int32).reshape(1),
        seg_lengths.reshape(1, -1),
        gathered,
        col_block,
        comp_block,
    )
    maps = jnp.concatenate([first_part, second_part], axis=0)
    both = jnp.einsum("cf,tf->ct", maps, features, preferred_element_type=jnp.float32)
    last = jnp.einsum("cf,tf->ct", first_part, tail_part, preferred_element_type=jnp.float32)
    forward = jnp.concatenate([both[:comp_block, LAG:], last], axis=1)
    backward = both[comp_block:]
    lag_error = (forward - backward - offset[:, :1]) * validity[None, :]
    return (koopman_rows, lag_error)


def solution(mesh):
    in_specs = (P("tm", None), P())
    out_specs = (P("feat", None), P("feat", "tm"))
    return jax.shard_map(shards, mesh=mesh, in_specs=in_specs, out_specs=out_specs, check_vma=False)
```
